512 devices in a mesh: mode: 8 (over x, core), band: 64 (over z, y).
Axes of the slice: x: 4, y: 4, z: 16, core: 2. Of those that a mesh axis runs over, the one named last changes fastest.
Arguments:
- mode_field: bfloat16 [8, 4096, 2, 4096], P('mode', 'band'), may hold values from -4 to 4
- figure: bfloat16 [4096, 4096], P('band'), may hold values from -6 to 6
- target: bfloat16 [4096, 4096], P('band'), may hold values from 0 to 2
- footprint: int32 [64, 64], replicated, may hold values from 0 to 4095, as said below
- approach_tiles: bfloat16 [3, 2, 128, 128], replicated, may hold values from -0.21875 to 0.21875
- focus_tiles: bfloat16 [3, 2, 128, 128], replicated, may hold values from -0.21875 to 0.21875
Outputs:
- sensitivity: float32 [4096, 4096], P('band')
The draws below stay inside these ranges and needn't reach their ends.
Inputs may be any that keep to these rules, and one draw needn't show every extreme that they name: `footprint`: entry [d, j] is the surface tile band * 64 + block read by beam tile j of band d; for every beam band d and surface band s at most 2 entries of row d name band s, and some row reaches 2 in every draw.
All inputs are finite; a program needn't handle non-finite values.
Results may differ from the reference program's by a relative error of at most 0.0082.
Values may be sent and summed in bfloat16 or wider, within the bound.
No kernel may reach another device: no remote copies, remote signals or barrier semaphores. Data moves between devices by JAX's collectives and lax.ppermute only.
A program may use at most 64 MiB of HBM per device.

```python
import jax
import jax.numpy as jnp
from jax import lax

GRID_CELLS = 4096
TILE = 128
MIRROR_TILE = 64
MODES = 8
BAND_TOTAL = 64
BAND_ROWS = 64
MIRROR_BLOCKS = 64
CAP = 2


def draw_footprint(key, part):
    count_of_bands = BAND_TOTAL
    mirror_block_list = MIRROR_BLOCKS
    raw_start = jax.random.randint(jax.random.fold_in(key, 11), (count_of_bands,), 0, count_of_bands)
    start_band = raw_start * raw_start // count_of_bands
    start_band = start_band.at[count_of_bands - 1].set(count_of_bands - 1)
    shift_draw = jax.random.randint(jax.random.fold_in(key, 12), (count_of_bands,), 0, CAP)
    shift_draw = shift_draw * (jnp.arange(count_of_bands) > 0).astype(jnp.int32)
    column = jnp.arange(mirror_block_list, dtype=jnp.int32)
    advance = (column[None, :] + shift_draw[:, None]) // CAP
    source_band = (start_band[:, None] + advance) % count_of_bands
    source_block = jax.random.randint(jax.random.fold_in(key, 13), (count_of_bands, mirror_block_list), 0, mirror_block_list)
    return (source_band * mirror_block_list + source_block).astype(jnp.int32)


def steps_of(key, extent, split, smallest, top_value):
    factor_of = 1.0
    for axis_at, blocks in split:
        heights = jax.random.uniform(jax.random.fold_in(jax.random.fold_in(key, 6), axis_at), (blocks,), jnp.float32, smallest / len(split), top_value / len(split))
        factor_of = factor_of * jnp.repeat(jnp.exp(heights), extent[axis_at] // blocks).reshape((-1,) + (1,) * (len(extent) - 1 - axis_at))
    return factor_of


def scatter_about(own_key, extent, scale, most, cuts=(), held_as=jnp.bfloat16):
    result = scale * jax.random.normal(own_key, extent, jnp.float32)
    if cuts:
        result = result * steps_of(own_key, extent, cuts, -0.22, 0.18)
    return jnp.clip(result, -most, most).astype(held_as)


def setup_inputs(seed: int = 0) -> dict:
    key_list = jax.random.split(jax.random.key(seed), 7)
    mode_field = scatter_about(key_list[0], (MODES, GRID_CELLS, 2, GRID_CELLS), (1.0 / (2 * MODES) ** 0.5), 4.0, ((0, 8), (1, 64)))
    figure = scatter_about(key_list[1], (GRID_CELLS, GRID_CELLS), 0.5, 6.0, ((0, 64),))
    target = jnp.clip(2.0 * jax.random.uniform(key_list[2], (GRID_CELLS, GRID_CELLS), jnp.float32) ** steps_of(key_list[2], (GRID_CELLS, GRID_CELLS), ((0, 64),), -0.2, 0.2), 0.0, 2.0).astype(jnp.bfloat16)
    footprint = draw_footprint(jax.random.fold_in(key_list[6], 71), 0)
    approach_tiles = scatter_about(key_list[4], (3, 2, TILE, TILE), (6 * TILE) ** -0.5, 0.21875)
    focus_tiles = scatter_about(key_list[5], (3, 2, TILE, TILE), (6 * TILE) ** -0.5, 0.21875)
    return dict(mode_field=mode_field, figure=figure, target=target, footprint=footprint, approach_tiles=approach_tiles, focus_tiles=focus_tiles)


PHASE_FACTOR = 4.0


def real_kernels(tile_set):
    tile_set = tile_set.astype(jnp.float32)
    real_part = tile_set[:, 0]
    imag_part = tile_set[:, 1]
    upper = jnp.stack([real_part, imag_part], axis=2)
    lower = jnp.stack([-imag_part, real_part], axis=2)
    return jnp.stack([upper, lower], axis=1)


def banded(grid_field, kernels):
    count_of_rows, parts_count, length = grid_field.shape
    tile_width = kernels.shape[2]
    mirror_block_list = length // tile_width
    reshaped_field = grid_field.astype(jnp.float32).reshape(count_of_rows, parts_count, mirror_block_list, tile_width)
    padded = jnp.pad(reshaped_field, ((0, 0), (0, 0), (1, 1), (0, 0)))
    running = jnp.zeros((count_of_rows, parts_count, mirror_block_list, tile_width), jnp.float32)
    for offset in range(3):
        running = running + jnp.einsum("rcbk,ckel->rebl", padded[:, :, offset:offset + mirror_block_list], kernels[offset])
    return running.reshape(count_of_rows, parts_count, length)


def to_tiles(field_plane):
    return field_plane.reshape(BAND_TOTAL, BAND_ROWS, MIRROR_BLOCKS, MIRROR_TILE).transpose(0, 2, 1, 3).reshape(BAND_TOTAL * MIRROR_BLOCKS, BAND_ROWS, MIRROR_TILE)


def from_tiles(stacked_tiles):
    return stacked_tiles.reshape(BAND_TOTAL, MIRROR_BLOCKS, BAND_ROWS, MIRROR_TILE).transpose(0, 2, 1, 3).reshape(GRID_CELLS, GRID_CELLS)


def reference(mode_field, figure, target, footprint, approach_tiles, focus_tiles):
    approach = real_kernels(approach_tiles)
    focus = real_kernels(focus_tiles)
    adjoint = jnp.transpose(focus, (0, 3, 4, 1, 2))[::-1]
    flat_index = footprint.reshape(-1).astype(jnp.int32)
    picked = to_tiles(figure.astype(jnp.float32))[flat_index]
    phase_delay = PHASE_FACTOR * from_tiles(picked)
    cosine = jnp.cos(phase_delay)
    sine_part = jnp.sin(phase_delay)

    def forward(power_sum, one_mode):
        propagated = banded(one_mode, approach).astype(jnp.bfloat16)
        turned = jnp.transpose(propagated, (2, 1, 0))
        advanced = banded(turned, approach).astype(jnp.bfloat16)
        real_part = advanced[:, 0].astype(jnp.float32)
        imag_part = advanced[:, 1].astype(jnp.float32)
        screened = jnp.stack([real_part * cosine - imag_part * sine_part, real_part * sine_part + imag_part * cosine], axis=1).astype(jnp.bfloat16)
        detected = banded(screened, focus)
        return power_sum + jnp.sum(detected * detected, axis=1), screened

    intensity, screens = lax.scan(forward, jnp.zeros((GRID_CELLS, GRID_CELLS), jnp.float32), mode_field)
    residual = intensity - target.astype(jnp.float32)

    def backward(sens_sum, screened):
        detected = banded(screened, focus)
        detector_grad = (detected * residual[:, None, :]).astype(jnp.bfloat16)
        mirror_grad = banded(detector_grad, adjoint)
        real_part = screened[:, 0].astype(jnp.float32)
        imag_part = screened[:, 1].astype(jnp.float32)
        return sens_sum + 2.0 * PHASE_FACTOR * (mirror_grad[:, 1] * real_part - mirror_grad[:, 0] * imag_part), None

    beam_sens, _ = lax.scan(backward, jnp.zeros((GRID_CELLS, GRID_CELLS), jnp.float32), screens)
    beam_tiles = to_tiles(beam_sens)
    surface = jnp.zeros_like(beam_tiles).at[flat_index].add(beam_tiles)
    return from_tiles(surface)
```

```python
import functools

import jax
import jax.numpy as jnp
from jax import lax
from jax.experimental import pallas as pl
from jax.experimental.pallas import tpu as pltpu
from jax.sharding import PartitionSpec as P

TILE = 128
HALF = 64
MIRROR_TILE = 64
PHASE_FACTOR = 4.0
F32 = jnp.float32
BF16 = jnp.bfloat16


def whole(*_):
    return pl.BlockSpec(memory_space=pltpu.VMEM)


def write_weights(tiles_ref, w_ref, split):
    for o in range(3):
        re = tiles_ref[o, 0].astype(F32)
        im = tiles_ref[o, 1].astype(F32)
        upper = jnp.concatenate([re, im], axis=1).astype(BF16)
        lower = jnp.concatenate([-im, re], axis=1).astype(BF16)
        if split:
            w_ref[o, 0:64] = upper[0:64]
            w_ref[o, 64:128] = lower[0:64]
            w_ref[o, 128:192] = upper[64:128]
            w_ref[o, 192:256] = lower[64:128]
        else:
            w_ref[o, 0:128] = upper
            w_ref[o, 128:256] = lower


def banded_rows(x_ref, w_ref, row, count, rows, flip=False):
    total = None
    for o in range(3):
        x = x_ref[pl.ds(pl.multiple_of(row + o * rows, 64), count)]
        if flip:
            part = lax.dot_general(x, w_ref[2 - o], (((1,), (1,)), ((), ())), preferred_element_type=F32)
        else:
            part = jnp.dot(x, w_ref[o], preferred_element_type=F32)
        total = part if total is None else total + part
    return total


def first_kernel(field_ref, tiles_ref, out_ref, x_ref, w_ref):
    rows = field_ref.shape[1]
    count_tiles = field_ref.shape[3] // TILE
    write_weights(tiles_ref, w_ref, False)
    x_ref[0:rows] = jnp.zeros((rows, 256), BF16)
    x_ref[(count_tiles + 1) * rows : (count_tiles + 2) * rows] = jnp.zeros((rows, 256), BF16)

    def fill(j, carry):
        at = pl.ds(pl.multiple_of(j * TILE, TILE), TILE)
        to = pl.ds(pl.multiple_of((j + 1) * rows, 64), rows)
        both = field_ref[0, :, :, at].astype(F32)
        x_ref[to, 0:128] = both[:, 0].astype(BF16)
        x_ref[to, 128:256] = both[:, 1].astype(BF16)
        return carry

    lax.fori_loop(0, count_tiles, fill, 0, unroll=4)
    step = 4

    def chunk(q, carry):
        got = banded_rows(x_ref, w_ref, q * (step * rows), step * rows, rows)
        for t in range(step):
            mine = got[t * rows : (t + 1) * rows]
            stacked = jnp.concatenate([mine[:, 0:128], mine[:, 128:256]], axis=0)
            turned = jnp.transpose(stacked).astype(BF16)
            at = (q * step + t) * 2
            for h in range(2):
                out_ref[:, pl.ds(at + h, 1)] = turned[h * 64 : (h + 1) * 64].reshape(8, 1, 8, 128)
        return carry

    lax.fori_loop(0, count_tiles // step, chunk, 0)


def first_stage(field, tiles):
    rows, length = field.shape[1], field.shape[3]
    tiles_count = length // TILE
    return pl.pallas_call(
        first_kernel,
        out_shape=jax.ShapeDtypeStruct((8, length // 64, 8, 128), BF16),
        in_specs=[whole(), whole()],
        out_specs=whole(),
        scratch_shapes=[pltpu.VMEM(((tiles_count + 2) * rows, 256), BF16), pltpu.VMEM((3, 256, 256), BF16)],
        cost_estimate=pl.CostEstimate(flops=2 * rows * tiles_count * 768 * 256, bytes_accessed=1 << 21, transcendentals=0),
        name="first",
    )(field, tiles)


def half_of(x, want, lane):
    return jnp.where(want, pltpu.roll(x, 64, 1), x)


def heights_out_kernel(index_ref, mine_ref, figure_ref, out_ref, wide_ref):
    count = out_ref.shape[0]
    pairs = figure_ref.shape[1] // 128
    lane = lax.broadcasted_iota(jnp.int32, (8, 128), 1)
    for p in range(pairs):
        wide_ref[p] = figure_ref[:, p * 128 : (p + 1) * 128].astype(F32)

    def slot(d, carry):
        k0 = index_ref[0, d]
        k1 = index_ref[1, d]
        a = half_of(wide_ref[k0 // 2], k0 % 2 != 0, lane)
        b = half_of(wide_ref[k1 // 2], k1 % 2 != 1, lane)
        out_ref[d] = jnp.where(lane < 64, a, b).astype(BF16)
        return carry

    lax.fori_loop(0, count, slot, 0, unroll=8)


def heights_out(index, mine, figure):
    bands = figure.shape[1] // 64
    return pl.pallas_call(
        heights_out_kernel,
        out_shape=jax.ShapeDtypeStruct((bands, 8, 128), BF16),
        grid_spec=pltpu.PrefetchScalarGridSpec(
            num_scalar_prefetch=2,
            grid=(1,),
            in_specs=[pl.BlockSpec((8, figure.shape[1]), lambda g, index, mine: (mine[0], 0))],
            out_specs=pl.BlockSpec((bands, 8, 128), lambda g, index, mine: (0, 0, 0)),
            scratch_shapes=[pltpu.VMEM((figure.shape[1] // 128, 8, 128), F32)],
        ),
        name="heights_out",
    )(index, mine, figure)


def phase_kernel(index_ref, tiles_ref, cos_ref, sin_ref):
    lane = lax.broadcasted_iota(jnp.int32, (8, 128), 1)
    pairs = cos_ref.shape[0]

    def pair(p, carry):
        s0, c0 = index_ref[0, 2 * p], index_ref[1, 2 * p]
        s1, c1 = index_ref[0, 2 * p + 1], index_ref[1, 2 * p + 1]
        a = half_of(tiles_ref[s0].astype(F32), c0 != 0, lane)
        b = half_of(tiles_ref[s1].astype(F32), c1 != 1, lane)
        phase = PHASE_FACTOR * jnp.where(lane < 64, a, b)
        cos_ref[p] = jnp.cos(phase)
        sin_ref[p] = jnp.sin(phase)
        return carry

    lax.fori_loop(0, pairs, pair, 0, unroll=2)


def phases(index, tiles):
    pairs = tiles.shape[0] // 2
    return pl.pallas_call(
        phase_kernel,
        out_shape=[jax.ShapeDtypeStruct((pairs, 8, 128), F32)] * 2,
        in_specs=[pl.BlockSpec(memory_space=pltpu.SMEM), whole()],
        out_specs=[whole(), whole()],
        name="phases",
    )(index, tiles)


def second_kernel(index_ref, mine_ref, got_ref, approach_ref, focus_ref, cos_ref, sin_ref, target_ref, out_ref,
                  x_ref, y_ref, g_ref, wp_ref, wf_ref):
    pairs = cos_ref.shape[0]
    rows = 64
    write_weights(approach_ref, wp_ref, True)
    write_weights(focus_ref, wf_ref, False)
    blank = jnp.zeros((rows, 256), BF16)
    for ref in (x_ref, y_ref, g_ref):
        ref[0:rows] = blank
        ref[(pairs + 1) * rows : (pairs + 2) * rows] = blank

    def fill(p, carry):
        to = pl.ds(pl.multiple_of((p + 1) * rows, 64), rows)
        for h in range(2):
            x = got_ref[:, 2 * p + h].astype(F32).reshape(rows, 128)
            x_ref[to, h * 128 : (h + 1) * 128] = x.astype(BF16)
        return carry

    lax.fori_loop(0, pairs, fill, 0, unroll=4)
    step = 4

    def mirror(q, carry):
        row = q * (step * rows)
        a2 = banded_rows(x_ref, wp_ref, row, step * rows, rows).astype(BF16).astype(F32)
        re = a2[:, 0:128].reshape(step, 8, 8, 128)
        im = a2[:, 128:256].reshape(step, 8, 8, 128)
        cos = cos_ref[pl.ds(q * step, step)][:, None]
        sin = sin_ref[pl.ds(q * step, step)][:, None]
        to = pl.ds(pl.multiple_of(row + rows, 64), step * rows)
        y_ref[to, 0:128] = (re * cos - im * sin).reshape(step * rows, 128).astype(BF16)
        y_ref[to, 128:256] = (re * sin + im * cos).reshape(step * rows, 128).astype(BF16)
        return carry

    lax.fori_loop(0, pairs // step, mirror, 0)

    def detect(q, carry):
        row = q * (step * rows)
        a4 = banded_rows(y_ref, wf_ref, row, step * rows, rows)
        re = a4[:, 0:128].reshape(step, 8, 8, 128)
        im = a4[:, 128:256].reshape(step, 8, 8, 128)
        power = jnp.sum(re * re + im * im, axis=1)
        to = pl.ds(pl.multiple_of(row + rows, 64), step * rows)
        for t in range(step):
            at = pl.ds(pl.multiple_of((q * step + t) * 128, 128), 128)
            left = (power[t] - target_ref[:, at].astype(F32))[None]
            to = pl.ds(pl.multiple_of(row + rows + t * rows, 64), rows)
            g_ref[to, 0:128] = (re[t] * left).reshape(rows, 128).astype(BF16)
            g_ref[to, 128:256] = (im[t] * left).reshape(rows, 128).astype(BF16)
        return carry

    lax.fori_loop(0, pairs // step, detect, 0)
    lane = lax.broadcasted_iota(jnp.int32, (8, 128), 1)
    out_ref[...] = jnp.zeros_like(out_ref)

    def adjoint(q, carry):
        row = q * (step * rows)
        g3 = banded_rows(g_ref, wf_ref, row, step * rows, rows, flip=True)
        own = pl.ds(pl.multiple_of(row + rows, 64), step * rows)
        re = y_ref[own, 0:128].astype(F32)
        im = y_ref[own, 128:256].astype(F32)
        terms = g3[:, 128:256] * re - g3[:, 0:128] * im
        sens = 2.0 * PHASE_FACTOR * jnp.sum(terms.reshape(step, 8, 8, 128), axis=1)
        for t in range(step):
            turned = pltpu.roll(sens[t], 64, 1)
            for h in range(2):
                j = (q * step + t) * 2 + h
                s, c = index_ref[0, j], index_ref[1, j]
                tile = jnp.where(c != h, turned, sens[t])
                out_ref[s] = jnp.where((lane < 64) == (c == 0), tile, out_ref[s].astype(F32)).astype(BF16)
        return carry

    lax.fori_loop(0, pairs // step, adjoint, 0)


def second_stage(index, mine, got, approach, focus, cos, sin, target):
    bands = got.shape[1]
    pairs = bands // 2
    keep = lambda *shape: pl.BlockSpec(shape, lambda g, index, mine: (0,) * len(shape))
    return pl.pallas_call(
        second_kernel,
        out_shape=jax.ShapeDtypeStruct((bands, 8, 128), BF16),
        grid_spec=pltpu.PrefetchScalarGridSpec(
            num_scalar_prefetch=2,
            grid=(1,),
            in_specs=[
                keep(*got.shape),
                keep(*approach.shape),
                keep(*focus.shape),
                keep(*cos.shape),
                keep(*sin.shape),
                pl.BlockSpec((8, target.shape[1]), lambda g, index, mine: (mine[0], 0)),
            ],
            out_specs=keep(bands, 8, 128),
            scratch_shapes=[pltpu.VMEM(((pairs + 2) * 64, 256), BF16)] * 3 + [pltpu.VMEM((3, 256, 256), BF16)] * 2,
        ),
        cost_estimate=pl.CostEstimate(flops=6 * 64 * pairs * 768 * 256, bytes_accessed=1 << 20, transcendentals=0),
        name="second",
    )(index, mine, got, approach, focus, cos, sin, target)


def collect_kernel(index_ref, tiles_ref, out_ref, sum_ref):
    lane = lax.broadcasted_iota(jnp.int32, (8, 128), 1)
    pairs = out_ref.shape[1] // 128
    sum_ref[...] = jnp.zeros_like(sum_ref)

    def slot(d, carry):
        x = tiles_ref[d].astype(F32)
        turned = pltpu.roll(x, 64, 1)
        for c in range(2):
            k = index_ref[c, d]
            tile = jnp.where(k % 2 != c, turned, x)
            sum_ref[k // 2] += jnp.where((lane < 64) == (k % 2 == 0), tile, 0.0)
        return carry

    lax.fori_loop(0, tiles_ref.shape[0], slot, 0, unroll=8)
    for p in range(pairs):
        out_ref[:, p * 128 : (p + 1) * 128] = sum_ref[p].astype(out_ref.dtype)


def collect(index, tiles, dtype):
    bands = tiles.shape[0]
    return pl.pallas_call(
        collect_kernel,
        out_shape=jax.ShapeDtypeStruct((8, bands * 64), dtype),
        in_specs=[pl.BlockSpec(memory_space=pltpu.SMEM), whole()],
        out_specs=whole(),
        scratch_shapes=[pltpu.VMEM((bands // 2 + 1, 8, 128), F32)],
        name="collect",
    )(index, tiles)


def shards(mode_field, figure, target, footprint, approach_tiles, focus_tiles):
    band = lax.axis_index("band")
    mine = lax.axis_index("mode").astype(jnp.int32).reshape(1)
    blocks = footprint.shape[1]
    source_band = footprint // blocks
    code = lax.broadcasted_iota(jnp.int32, footprint.shape, 1) * blocks + footprint % blocks
    here = source_band == band
    low = jnp.min(jnp.where(here, code, blocks * blocks), axis=1)
    high = jnp.max(jnp.where(here, code, -1), axis=1)
    send_index = jnp.stack([jnp.where(high >= 0, low % blocks, 0), jnp.maximum(high, 0) % blocks])
    add_index = jnp.stack([jnp.where(high >= 0, low % blocks, blocks), jnp.where(high > low, high % blocks, blocks)])
    my_band = lax.dynamic_index_in_dim(source_band, band, 0, keepdims=False)
    column = jnp.arange(blocks, dtype=jnp.int32)
    same = (my_band[:, None] == my_band[None, :]) & (column[None, :] < column[:, None])
    beam_index = jnp.stack([my_band, jnp.any(same, axis=1).astype(jnp.int32)])

    heights = heights_out(send_index, mine, figure)
    heights = lax.all_to_all(heights, "band", split_axis=0, concat_axis=0, tiled=True)
    out = first_stage(mode_field, approach_tiles)
    got = lax.all_to_all(out.reshape(-1, 8, 128), ("mode", "band"), split_axis=0, concat_axis=0, tiled=True)
    cos, sin = phases(beam_index, heights)
    got = got.reshape(out.shape)
    tiles = second_stage(beam_index, mine, got, approach_tiles, focus_tiles, cos, sin, target)
    tiles = lax.all_to_all(tiles, "band", split_axis=0, concat_axis=0, tiled=True)
    own = collect(add_index, tiles, BF16)
    return lax.all_gather(own, "mode", axis=0, tiled=True).astype(F32)


def solution(mesh):
    in_specs = (P("mode", "band", None, None), P("band", None), P("band", None), P(), P(), P())
    out_specs = P("band", None)
    return jax.shard_map(shards, mesh=mesh, in_specs=in_specs, out_specs=out_specs, check_vma=False)
```

```python
import jax
import jax.numpy as jnp
from jax import lax
from jax.experimental import pallas as pl
from jax.experimental.pallas import tpu as pltpu
from jax.sharding import PartitionSpec as P


TILE = 128
PHASE_FACTOR = 4.0
F32 = jnp.float32
BF16 = jnp.bfloat16


def whole(*_):
    return pl.BlockSpec(memory_space=pltpu.VMEM)


def write_weights(tiles_ref, w_ref, split):
    for o in range(3):
        re = tiles_ref[o, 0].astype(F32)
        im = tiles_ref[o, 1].astype(F32)
        upper = jnp.concatenate([re, im], axis=1).astype(BF16)
        lower = jnp.concatenate([-im, re], axis=1).astype(BF16)
        if split:
            w_ref[o, 0:64] = upper[0:64]
            w_ref[o, 64:128] = lower[0:64]
            w_ref[o, 128:192] = upper[64:128]
            w_ref[o, 192:256] = lower[64:128]
        else:
            w_ref[o, 0:128] = upper
            w_ref[o, 128:256] = lower


def banded_rows(x_ref, w_ref, row, count, rows, flip=False):
    total = None
    for o in range(3):
        x = x_ref[pl.ds(pl.multiple_of(row + o * rows, 64), count)]
        if flip:
            part = lax.dot_general(x, w_ref[2 - o], (((1,), (1,)), ((), ())), preferred_element_type=F32)
        else:
            part = jnp.dot(x, w_ref[o], preferred_element_type=F32)
        total = part if total is None else total + part
    return total


def first_kernel(field_ref, tiles_ref, out_ref, x_ref, w_ref):
    rows = field_ref.shape[1]
    count_tiles = field_ref.shape[3] // TILE
    write_weights(tiles_ref, w_ref, False)
    x_ref[0:rows] = jnp.zeros((rows, 256), BF16)
    x_ref[(count_tiles + 1) * rows : (count_tiles + 2) * rows] = jnp.zeros((rows, 256), BF16)

    def fill(j, carry):
        at = pl.ds(pl.multiple_of(j * TILE, TILE), TILE)
        to = pl.ds(pl.multiple_of((j + 1) * rows, 64), rows)
        both = field_ref[0, :, :, at].astype(F32)
        x_ref[to, 0:128] = both[:, 0].astype(BF16)
        x_ref[to, 128:256] = both[:, 1].astype(BF16)
        return carry

    lax.fori_loop(0, count_tiles, fill, 0, unroll=4)
    step = 4

    def chunk(q, carry):
        got = banded_rows(x_ref, w_ref, q * (step * rows), step * rows, rows)
        for t in range(step):
            mine = got[t * rows : (t + 1) * rows]
            stacked = jnp.concatenate([mine[:, 0:128], mine[:, 128:256]], axis=0)
            turned = jnp.transpose(stacked).astype(BF16)
            at = (q * step + t) * 2
            for h in range(2):
                out_ref[:, pl.ds(at + h, 1)] = turned[h * 64 : (h + 1) * 64].reshape(8, 1, 8, 128)
        return carry

    lax.fori_loop(0, count_tiles // step, chunk, 0)


def first_stage(field, tiles):
    rows, length = field.shape[1], field.shape[3]
    tiles_count = length // TILE
    return pl.pallas_call(
        first_kernel,
        out_shape=jax.ShapeDtypeStruct((8, length // 64, 8, 128), BF16),
        in_specs=[whole(), whole()],
        out_specs=whole(),
        scratch_shapes=[pltpu.VMEM(((tiles_count + 2) * rows, 256), BF16), pltpu.VMEM((3, 256, 256), BF16)],
        cost_estimate=pl.CostEstimate(flops=2 * rows * tiles_count * 768 * 256, bytes_accessed=1 << 21, transcendentals=0),
        name="first",
    )(field, tiles)


def half_of(x, want):
    return jnp.where(want, pltpu.roll(x, 64, 1), x)


def heights_out_kernel(index_ref, mine_ref, figure_ref, *refs):
    outs, wide_ref = refs[:4], refs[4]
    pairs = figure_ref.shape[1] // 128
    lane = lax.broadcasted_iota(jnp.int32, (8, 128), 1)
    for p in range(pairs):
        wide_ref[p] = figure_ref[:, p * 128 : (p + 1) * 128].astype(F32)

    z, y = mine_ref[1], mine_ref[2]
    for low in range(4):

        def slot(at, carry):
            d = ((z + 4 * (at >> 2) + low + 11) & 15) * 4 + ((y + at + 3) & 3)
            k0 = index_ref[0, d]
            k1 = index_ref[1, d]
            a = half_of(wide_ref[k0 >> 1], (k0 & 1) != 0)
            b = half_of(wide_ref[k1 >> 1], (k1 & 1) != 1)
            outs[low][at] = jnp.where(lane < 64, a, b).astype(BF16)
            return carry

        lax.fori_loop(0, 16, slot, 0, unroll=8)


def heights_out(index, mine, figure):
    out = pl.BlockSpec((16, 8, 128), lambda g, index, mine: (0, 0, 0))
    return pl.pallas_call(
        heights_out_kernel,
        out_shape=[jax.ShapeDtypeStruct((16, 8, 128), BF16)] * 4,
        grid_spec=pltpu.PrefetchScalarGridSpec(
            num_scalar_prefetch=2,
            grid=(1,),
            in_specs=[pl.BlockSpec((8, figure.shape[1]), lambda g, index, mine: (mine[0], 0))],
            out_specs=[out] * 4,
            scratch_shapes=[pltpu.VMEM((figure.shape[1] // 128, 8, 128), F32)],
        ),
        name="heights_out",
    )(index, mine, figure)


def regroup_kernel(*refs):
    for a in range(4):
        for b in range(4):
            refs[4 + b][4 * a : 4 * a + 4] = refs[a][4 * b : 4 * b + 4]


def regroup(parts):
    return pl.pallas_call(
        regroup_kernel,
        out_shape=[jax.ShapeDtypeStruct(parts[0].shape, BF16)] * 4,
        in_specs=[whole()] * 4,
        out_specs=[whole()] * 4,
        name="regroup",
    )(*parts)


def regroup_last_kernel(*refs):
    for b in range(4):
        for a in range(4):
            for c in range(4):
                refs[4 + c][4 * a + b] = refs[b][4 * a + c]


def regroup_last(parts):
    return pl.pallas_call(
        regroup_last_kernel,
        out_shape=[jax.ShapeDtypeStruct(parts[0].shape, BF16)] * 4,
        in_specs=[whole()] * 4,
        out_specs=[whole()] * 4,
        name="regroup_last",
    )(*parts)


DIGITS = (-1, 0, 1, 2)


def moved(parts, bands, way):
    spots = bands // 4

    def target(b, step):
        z, y = b // 4, b % 4
        if way == "low":
            return (z + step) % spots * 4 + y
        if way == "high":
            return (z + 4 * step) % spots * 4 + y
        return z * 4 + (y + step) % 4

    return [
        part if step == 0 else lax.ppermute(part, "band", [(b, target(b, step)) for b in range(bands)])
        for part, step in zip(parts, DIGITS)
    ]


def phase_kernel(index_ref, *refs):
    cos_ref, sin_ref, wide_ref = refs[4:]
    lane = lax.broadcasted_iota(jnp.int32, (8, 128), 1)
    pairs = cos_ref.shape[0]
    for a in range(4):
        for b in range(16):
            wide_ref[16 * a + b] = refs[a][b].astype(F32)

    def pair(p, carry):
        s0, c0 = index_ref[0, 2 * p], index_ref[1, 2 * p]
        s1, c1 = index_ref[0, 2 * p + 1], index_ref[1, 2 * p + 1]
        a = half_of(wide_ref[s0], c0 != 0)
        b = half_of(wide_ref[s1], c1 != 1)
        phase = PHASE_FACTOR * jnp.where(lane < 64, a, b)
        cos_ref[p] = jnp.cos(phase)
        sin_ref[p] = jnp.sin(phase)
        return carry

    lax.fori_loop(0, pairs, pair, 0, unroll=2)


def phases(index, parts, pairs):
    return pl.pallas_call(
        phase_kernel,
        out_shape=[jax.ShapeDtypeStruct((pairs, 8, 128), F32)] * 2,
        in_specs=[pl.BlockSpec(memory_space=pltpu.SMEM)] + [whole()] * 4,
        out_specs=[whole(), whole()],
        scratch_shapes=[pltpu.VMEM((64, 8, 128), F32)],
        name="phases",
    )(index, *parts)


def second_kernel(index_ref, mine_ref, got_ref, approach_ref, focus_ref, cos_ref, sin_ref, target_ref, out_ref,
                  x_ref, y_ref, g_ref, wp_ref, wf_ref):
    pairs = cos_ref.shape[0]
    rows = 64
    write_weights(approach_ref, wp_ref, True)
    write_weights(focus_ref, wf_ref, False)
    blank = jnp.zeros((rows, 256), BF16)
    for ref in (x_ref, y_ref, g_ref):
        ref[0:rows] = blank
        ref[(pairs + 1) * rows : (pairs + 2) * rows] = blank

    def fill(p, carry):
        to = pl.ds(pl.multiple_of((p + 1) * rows, 64), rows)
        for h in range(2):
            x = got_ref[:, 2 * p + h].astype(F32).reshape(rows, 128)
            x_ref[to, h * 128 : (h + 1) * 128] = x.astype(BF16)
        return carry

    lax.fori_loop(0, pairs, fill, 0, unroll=4)
    step = 4

    def mirror(q, carry):
        row = q * (step * rows)
        a2 = banded_rows(x_ref, wp_ref, row, step * rows, rows).astype(BF16).astype(F32)
        re = a2[:, 0:128].reshape(step, 8, 8, 128)
        im = a2[:, 128:256].reshape(step, 8, 8, 128)
        cos = cos_ref[pl.ds(q * step, step)][:, None]
        sin = sin_ref[pl.ds(q * step, step)][:, None]
        to = pl.ds(pl.multiple_of(row + rows, 64), step * rows)
        y_ref[to, 0:128] = (re * cos - im * sin).reshape(step * rows, 128).astype(BF16)
        y_ref[to, 128:256] = (re * sin + im * cos).reshape(step * rows, 128).astype(BF16)
        return carry

    lax.fori_loop(0, pairs // step, mirror, 0)

    def detect(q, carry):
        row = q * (step * rows)
        a4 = banded_rows(y_ref, wf_ref, row, step * rows, rows)
        re = a4[:, 0:128].reshape(step, 8, 8, 128)
        im = a4[:, 128:256].reshape(step, 8, 8, 128)
        power = jnp.sum(re * re + im * im, axis=1)
        to = pl.ds(pl.multiple_of(row + rows, 64), step * rows)
        for t in range(step):
            at = pl.ds(pl.multiple_of((q * step + t) * 128, 128), 128)
            left = (power[t] - target_ref[:, at].astype(F32))[None]
            to = pl.ds(pl.multiple_of(row + rows + t * rows, 64), rows)
            g_ref[to, 0:128] = (re[t] * left).reshape(rows, 128).astype(BF16)
            g_ref[to, 128:256] = (im[t] * left).reshape(rows, 128).astype(BF16)
        return carry

    lax.fori_loop(0, pairs // step, detect, 0)
    lane = lax.broadcasted_iota(jnp.int32, (8, 128), 1)
    out_ref[...] = jnp.zeros_like(out_ref)

    def adjoint(q, carry):
        row = q * (step * rows)
        g3 = banded_rows(g_ref, wf_ref, row, step * rows, rows, flip=True)
        own = pl.ds(pl.multiple_of(row + rows, 64), step * rows)
        re = y_ref[own, 0:128].astype(F32)
        im = y_ref[own, 128:256].astype(F32)
        terms = g3[:, 128:256] * re - g3[:, 0:128] * im
        sens = 2.0 * PHASE_FACTOR * jnp.sum(terms.reshape(step, 8, 8, 128), axis=1)
        for t in range(step):
            turned = pltpu.roll(sens[t], 64, 1)
            for h in range(2):
                j = (q * step + t) * 2 + h
                s, c = index_ref[0, j], index_ref[1, j]
                tile = jnp.where(c != h, turned, sens[t])
                out_ref[s] = jnp.where((lane < 64) == (c == 0), tile, out_ref[s].astype(F32)).astype(BF16)
        return carry

    lax.fori_loop(0, pairs // step, adjoint, 0)


def second_stage(index, mine, got, approach, focus, cos, sin, target):
    bands = got.shape[1]
    pairs = bands // 2
    keep = lambda *shape: pl.BlockSpec(shape, lambda g, index, mine: (0,) * len(shape))
    return pl.pallas_call(
        second_kernel,
        out_shape=jax.ShapeDtypeStruct((bands, 8, 128), BF16),
        grid_spec=pltpu.PrefetchScalarGridSpec(
            num_scalar_prefetch=2,
            grid=(1,),
            in_specs=[
                keep(*got.shape),
                keep(*approach.shape),
                keep(*focus.shape),
                keep(*cos.shape),
                keep(*sin.shape),
                pl.BlockSpec((8, target.shape[1]), lambda g, index, mine: (mine[0], 0)),
            ],
            out_specs=keep(bands, 8, 128),
            scratch_shapes=[pltpu.VMEM(((pairs + 2) * 64, 256), BF16)] * 3 + [pltpu.VMEM((3, 256, 256), BF16)] * 2,
        ),
        cost_estimate=pl.CostEstimate(flops=6 * 64 * pairs * 768 * 256, bytes_accessed=1 << 20, transcendentals=0),
        name="second",
    )(index, mine, got, approach, focus, cos, sin, target)


def collect_kernel(index_ref, tiles_ref, out_ref, sum_ref):
    lane = lax.broadcasted_iota(jnp.int32, (8, 128), 1)
    pairs = out_ref.shape[1] // 128
    sum_ref[...] = jnp.zeros_like(sum_ref)

    def slot(d, carry):
        x = tiles_ref[d].astype(F32)
        turned = pltpu.roll(x, 64, 1)
        for c in range(2):
            k = index_ref[c, d]
            tile = jnp.where((k & 1) != c, turned, x)
            sum_ref[k >> 1] += jnp.where((lane < 64) == ((k & 1) == 0), tile, 0.0)
        return carry

    lax.fori_loop(0, tiles_ref.shape[0], slot, 0, unroll=8)
    for p in range(pairs):
        out_ref[:, p * 128 : (p + 1) * 128] = sum_ref[p].astype(out_ref.dtype)


def collect(index, tiles, dtype):
    bands = tiles.shape[0]
    return pl.pallas_call(
        collect_kernel,
        out_shape=jax.ShapeDtypeStruct((8, bands * 64), dtype),
        in_specs=[pl.BlockSpec(memory_space=pltpu.SMEM), whole()],
        out_specs=whole(),
        scratch_shapes=[pltpu.VMEM((bands // 2 + 1, 8, 128), F32)],
        name="collect",
    )(index, tiles)


def shards(mode_field, figure, target, footprint, approach_tiles, focus_tiles):
    band = lax.axis_index("band").astype(jnp.int32)
    z, y = band >> 2, band & 3
    mine = jnp.stack([lax.axis_index("mode").astype(jnp.int32), z, y])
    bands, blocks = footprint.shape
    out = first_stage(mode_field, approach_tiles)
    got = lax.all_to_all(out.reshape(-1, 8, 128), ("mode", "band"), split_axis=0, concat_axis=0, tiled=True)
    got = got.reshape(out.shape)
    source_band = lax.div(footprint, blocks)
    code = lax.broadcasted_iota(jnp.int32, footprint.shape, 1) * blocks + lax.rem(footprint, blocks)
    here = source_band == band
    low = jnp.min(jnp.where(here, code, blocks * blocks), axis=1)
    high = jnp.max(jnp.where(here, code, -1), axis=1)
    add_index = jnp.stack([jnp.where(high >= 0, low & (blocks - 1), blocks), jnp.where(high > low, high & (blocks - 1), blocks)])
    my_band = lax.dynamic_index_in_dim(source_band, band, 0, keepdims=False)
    column = jnp.arange(blocks, dtype=jnp.int32)
    same = (my_band[:, None] == my_band[None, :]) & (column[None, :] < column[:, None])
    my_slot = jnp.any(same, axis=1).astype(jnp.int32)
    beam_index = jnp.stack([my_band, my_slot])
    dz = z - (my_band >> 2)
    step_low = (dz + 1) & 3
    step_high = (((dz + 1 - step_low) >> 2) + 1) & 3
    step_y = (y - my_band + 1) & 3
    read_index = jnp.stack([16 * step_y + 4 * step_low + step_high, my_slot])
    parts = heights_out(add_index & (blocks - 1), mine, figure)
    parts = moved(parts, bands, "low")
    parts = regroup(parts)
    parts = moved(parts, bands, "high")
    parts = regroup_last(parts)
    parts = moved(parts, bands, "y")
    cos, sin = phases(read_index, parts, bands // 2)
    tiles = second_stage(beam_index, mine, got, approach_tiles, focus_tiles, cos, sin, target)
    tiles = lax.all_to_all(tiles, "band", split_axis=0, concat_axis=0, tiled=True)
    own = collect(add_index, tiles, BF16)
    return lax.all_gather(own, "mode", axis=0, tiled=True).astype(F32)


def solution(mesh):
    in_specs = (P("mode", "band", None, None), P("band", None), P("band", None), P(), P(), P())
    out_specs = P("band", None)
    return jax.shard_map(shards, mesh=mesh, in_specs=in_specs, out_specs=out_specs, check_vma=False)
```

```python
import jax
import jax.numpy as jnp
from jax import lax
from jax.experimental import pallas as pl
from jax.experimental.pallas import tpu as pltpu
from jax.sharding import PartitionSpec as P


TILE = 128
PHASE_FACTOR = 4.0
F32 = jnp.float32
BF16 = jnp.bfloat16


def whole(*_):
    return pl.BlockSpec(memory_space=pltpu.VMEM)


def write_weights(tiles_ref, w_ref, split):
    for o in range(3):
        re = tiles_ref[o, 0].astype(F32)
        im = tiles_ref[o, 1].astype(F32)
        upper = jnp.concatenate([re, im], axis=1).astype(BF16)
        lower = jnp.concatenate([-im, re], axis=1).astype(BF16)
        if split:
            w_ref[o, 0:64] = upper[0:64]
            w_ref[o, 64:128] = lower[0:64]
            w_ref[o, 128:192] = upper[64:128]
            w_ref[o, 192:256] = lower[64:128]
        else:
            w_ref[o, 0:128] = upper
            w_ref[o, 128:256] = lower


def banded_rows(x_ref, w_ref, row, count, rows, flip=False):
    total = None
    for o in range(3):
        x = x_ref[pl.ds(pl.multiple_of(row + o * rows, 64), count)]
        if flip:
            part = lax.dot_general(x, w_ref[2 - o], (((1,), (1,)), ((), ())), preferred_element_type=F32)
        else:
            part = jnp.dot(x, w_ref[o], preferred_element_type=F32)
        total = part if total is None else total + part
    return total


def first_kernel(field_ref, tiles_ref, out_ref, wide_ref, x_ref, w_ref):
    rows = x_ref.shape[0] // (field_ref.shape[0] // 128 + 2)
    count_tiles = field_ref.shape[0] // 128
    write_weights(tiles_ref, w_ref, False)
    x_ref[0:rows] = jnp.zeros((rows, 256), BF16)
    x_ref[(count_tiles + 1) * rows : (count_tiles + 2) * rows] = jnp.zeros((rows, 256), BF16)
    for u in range(rows):
        wide_ref[u * 65 : u * 65 + 64] = field_ref[u * 64 : (u + 1) * 64].astype(F32)
    for j in range(count_tiles):
        for c in range(2):
            x_ref[(j + 1) * rows : (j + 2) * rows, c * 128 : (c + 1) * 128] = wide_ref[
                pl.ds(2 * j + c, rows, stride=65)
            ].astype(BF16)
    step = 16

    def chunk(q, carry):
        got = banded_rows(x_ref, w_ref, q * (step * rows), step * rows, rows)
        for t in range(step):
            mine = got[t * rows : (t + 1) * rows]
            stacked = jnp.concatenate([mine[:, 0:128], mine[:, 128:256]], axis=0)
            turned = jnp.transpose(stacked).astype(BF16)
            at = (q * step + t) * 2
            for h in range(2):
                out_ref[:, pl.ds(at + h, 1)] = turned[h * 64 : (h + 1) * 64].reshape(8, 1, 8, 128)
        return carry

    lax.fori_loop(0, count_tiles // step, chunk, 0)


def first_stage(field, tiles):
    rows, length = field.shape[1], field.shape[3]
    tiles_count = length // TILE
    field = field.reshape(rows, 2, tiles_count, TILE).transpose(0, 2, 1, 3).reshape(rows * tiles_count * 2, TILE)
    return pl.pallas_call(
        first_kernel,
        out_shape=jax.ShapeDtypeStruct((8, length // 64, 8, 128), BF16),
        in_specs=[whole(), whole()],
        out_specs=whole(),
        scratch_shapes=[
            pltpu.VMEM((64 * 65, 128), F32),
            pltpu.VMEM(((tiles_count + 2) * rows, 256), BF16),
            pltpu.VMEM((3, 256, 256), BF16),
        ],
        cost_estimate=pl.CostEstimate(flops=2 * rows * tiles_count * 768 * 256, bytes_accessed=1 << 21, transcendentals=0),
        name="first",
    )(field, tiles)


def both_ways(wide_ref, at, x):
    wide_ref[2 * at] = x
    wide_ref[2 * at + 1] = pltpu.roll(x, 64, 1)


def heights_out_kernel(index_ref, mine_ref, figure_ref, *refs):
    outs, wide_ref = refs[:4], refs[4]
    pairs = figure_ref.shape[1] // 128
    lane = lax.broadcasted_iota(jnp.int32, (8, 128), 1)
    for p in range(pairs):
        both_ways(wide_ref, p, figure_ref[:, p * 128 : (p + 1) * 128].astype(F32))
    z, y = mine_ref[1], mine_ref[2]
    for leg in range(4):
        for at in range(16):
            d = ((z + at) & 15) * 4 + ((y + leg + 3) & 3)
            outs[leg][at] = jnp.where(lane < 64, wide_ref[index_ref[0, d]], wide_ref[index_ref[1, d]]).astype(BF16)


def heights_out(index, mine, figure):
    out = pl.BlockSpec((16, 8, 128), lambda g, index, mine: (0, 0, 0))
    return pl.pallas_call(
        heights_out_kernel,
        out_shape=[jax.ShapeDtypeStruct((16, 8, 128), BF16)] * 4,
        grid_spec=pltpu.PrefetchScalarGridSpec(
            num_scalar_prefetch=2,
            grid=(1,),
            in_specs=[pl.BlockSpec((8, figure.shape[1]), lambda g, index, mine: (mine[0], 0))],
            out_specs=[out] * 4,
            scratch_shapes=[pltpu.VMEM((figure.shape[1] // 64, 8, 128), F32)],
        ),
        name="heights_out",
    )(index, mine, figure)


def regroup_kernel(*refs):
    for y in range(4):
        for z in range(16):
            refs[4 + z][y] = refs[y][z]


def regroup(parts):
    return pl.pallas_call(
        regroup_kernel,
        out_shape=[jax.ShapeDtypeStruct((4, 8, 128), BF16)] * 16,
        in_specs=[whole()] * 4,
        out_specs=[whole()] * 16,
        name="regroup",
    )(*parts)


def moved(part, bands, z_step, y_step):
    spots = bands // 4
    if z_step == 0 and y_step == 0:
        return part
    target = lambda b: (b // 4 + z_step) % spots * 4 + (b + y_step) % 4
    return lax.ppermute(part, "band", [(b, target(b)) for b in range(bands)])


def phase_kernel(index_ref, *refs):
    cos_ref, sin_ref, wide_ref = refs[16:]
    lane = lax.broadcasted_iota(jnp.int32, (8, 128), 1)
    pairs = cos_ref.shape[0]
    for z in range(16):
        for y in range(4):
            both_ways(wide_ref, 4 * z + y, refs[z][y].astype(F32))

    def pair(p, carry):
        phase = PHASE_FACTOR * jnp.where(lane < 64, wide_ref[index_ref[2 * p]], wide_ref[index_ref[2 * p + 1]])
        cos_ref[p] = jnp.cos(phase)
        sin_ref[p] = jnp.sin(phase)
        return carry

    lax.fori_loop(0, pairs, pair, 0, unroll=4)


def phases(index, parts, pairs):
    return pl.pallas_call(
        phase_kernel,
        out_shape=[jax.ShapeDtypeStruct((pairs, 8, 128), F32)] * 2,
        in_specs=[pl.BlockSpec(memory_space=pltpu.SMEM)] + [whole()] * 16,
        out_specs=[whole(), whole()],
        scratch_shapes=[pltpu.VMEM((128, 8, 128), F32)],
        name="phases",
    )(index, *parts)


def second_kernel(index_ref, mine_ref, got_ref, approach_ref, focus_ref, cos_ref, sin_ref, target_ref, out_ref,
                  x_ref, y_ref, g_ref, wp_ref, wf_ref):
    pairs = cos_ref.shape[0]
    rows = 64
    write_weights(approach_ref, wp_ref, True)
    write_weights(focus_ref, wf_ref, False)
    blank = jnp.zeros((rows, 256), BF16)
    for ref in (x_ref, y_ref, g_ref):
        ref[0:rows] = blank
        ref[(pairs + 1) * rows : (pairs + 2) * rows] = blank

    def fill(p, carry):
        to = pl.ds(pl.multiple_of((p + 1) * rows, 64), rows)
        for h in range(2):
            x = got_ref[:, 2 * p + h].astype(F32).reshape(rows, 128)
            x_ref[to, h * 128 : (h + 1) * 128] = x.astype(BF16)
        return carry

    lax.fori_loop(0, pairs, fill, 0, unroll=4)
    step = 16

    def mirror(q, carry):
        row = q * (step * rows)
        a2 = banded_rows(x_ref, wp_ref, row, step * rows, rows).astype(BF16).astype(F32)
        re = a2[:, 0:128].reshape(step, 8, 8, 128)
        im = a2[:, 128:256].reshape(step, 8, 8, 128)
        cos = cos_ref[pl.ds(q * step, step)][:, None]
        sin = sin_ref[pl.ds(q * step, step)][:, None]
        to = pl.ds(pl.multiple_of(row + rows, 64), step * rows)
        y_ref[to, 0:128] = (re * cos - im * sin).reshape(step * rows, 128).astype(BF16)
        y_ref[to, 128:256] = (re * sin + im * cos).reshape(step * rows, 128).astype(BF16)
        return carry

    lax.fori_loop(0, pairs // step, mirror, 0)

    def detect(q, carry):
        row = q * (step * rows)
        a4 = banded_rows(y_ref, wf_ref, row, step * rows, rows)
        re = a4[:, 0:128].reshape(step, 8, 8, 128)
        im = a4[:, 128:256].reshape(step, 8, 8, 128)
        power = jnp.sum(re * re + im * im, axis=1)
        to = pl.ds(pl.multiple_of(row + rows, 64), step * rows)
        for t in range(step):
            at = pl.ds(pl.multiple_of((q * step + t) * 128, 128), 128)
            left = (power[t] - target_ref[:, at].astype(F32))[None]
            to = pl.ds(pl.multiple_of(row + rows + t * rows, 64), rows)
            g_ref[to, 0:128] = (re[t] * left).reshape(rows, 128).astype(BF16)
            g_ref[to, 128:256] = (im[t] * left).reshape(rows, 128).astype(BF16)
        return carry

    lax.fori_loop(0, pairs // step, detect, 0)
    lane = lax.broadcasted_iota(jnp.int32, (8, 128), 1)
    out_ref[...] = jnp.zeros_like(out_ref)

    def adjoint(q, carry):
        row = q * (step * rows)
        g3 = banded_rows(g_ref, wf_ref, row, step * rows, rows, flip=True)
        own = pl.ds(pl.multiple_of(row + rows, 64), step * rows)
        re = y_ref[own, 0:128].astype(F32)
        im = y_ref[own, 128:256].astype(F32)
        terms = g3[:, 128:256] * re - g3[:, 0:128] * im
        sens = 2.0 * PHASE_FACTOR * jnp.sum(terms.reshape(step, 8, 8, 128), axis=1)
        for t in range(step):
            turned = pltpu.roll(sens[t], 64, 1)
            for h in range(2):
                j = (q * step + t) * 2 + h
                s, c = index_ref[0, j], index_ref[1, j]
                tile = jnp.where(c != h, turned, sens[t])
                out_ref[s] = jnp.where((lane < 64) == (c == 0), tile, out_ref[s].astype(F32)).astype(BF16)
        return carry

    lax.fori_loop(0, pairs // step, adjoint, 0)


def second_stage(index, mine, got, approach, focus, cos, sin, target):
    bands = got.shape[1]
    pairs = bands // 2
    keep = lambda *shape: pl.BlockSpec(shape, lambda g, index, mine: (0,) * len(shape))
    return pl.pallas_call(
        second_kernel,
        out_shape=jax.ShapeDtypeStruct((bands, 8, 128), BF16),
        grid_spec=pltpu.PrefetchScalarGridSpec(
            num_scalar_prefetch=2,
            grid=(1,),
            in_specs=[
                keep(*got.shape),
                keep(*approach.shape),
                keep(*focus.shape),
                keep(*cos.shape),
                keep(*sin.shape),
                pl.BlockSpec((8, target.shape[1]), lambda g, index, mine: (mine[0], 0)),
            ],
            out_specs=keep(bands, 8, 128),
            scratch_shapes=[pltpu.VMEM(((pairs + 2) * 64, 256), BF16)] * 3 + [pltpu.VMEM((3, 256, 256), BF16)] * 2,
        ),
        cost_estimate=pl.CostEstimate(flops=6 * 64 * pairs * 768 * 256, bytes_accessed=1 << 20, transcendentals=0),
        name="second",
    )(index, mine, got, approach, focus, cos, sin, target)


def collect_kernel(index_ref, tiles_ref, out_ref, wide_ref, *sums):
    lane = lax.broadcasted_iota(jnp.int32, (8, 128), 1)
    pairs = out_ref.shape[2] // 128
    bands = tiles_ref.shape[0]
    for part in sums:
        part[...] = jnp.zeros_like(part)
    for d in range(bands):
        both_ways(wide_ref, d, tiles_ref[d].astype(F32))
    for d in range(bands):
        for c in range(2):
            part = sums[2 * (d % 2) + c]
            k = index_ref[c, d]
            part[k] += wide_ref[2 * d + ((k & 1) ^ c)]
    for p in range(pairs):
        low = sums[0][2 * p] + sums[1][2 * p] + sums[2][2 * p] + sums[3][2 * p]
        high = sums[0][2 * p + 1] + sums[1][2 * p + 1] + sums[2][2 * p + 1] + sums[3][2 * p + 1]
        tile = jnp.where(lane < 64, low, high).astype(out_ref.dtype)
        for copy in range(out_ref.shape[0]):
            out_ref[copy, :, p * 128 : (p + 1) * 128] = tile


def collect(index, tiles, copies, dtype):
    bands = tiles.shape[0]
    return pl.pallas_call(
        collect_kernel,
        out_shape=jax.ShapeDtypeStruct((copies, 8, bands * 64), dtype),
        in_specs=[pl.BlockSpec(memory_space=pltpu.SMEM), whole()],
        out_specs=whole(),
        scratch_shapes=[pltpu.VMEM((2 * bands, 8, 128), F32)] + [pltpu.VMEM((bands + 8, 8, 128), F32)] * 4,
        name="collect",
    )(index, tiles)


def shards(mode_field, figure, target, footprint, approach_tiles, focus_tiles):
    band = lax.axis_index("band").astype(jnp.int32)
    z, y = band >> 2, band & 3
    mine = jnp.stack([lax.axis_index("mode").astype(jnp.int32), z, y])
    bands, blocks = footprint.shape
    out = first_stage(mode_field, approach_tiles)
    got = lax.all_to_all(out.reshape(-1, 8, 128), ("mode", "band"), split_axis=0, concat_axis=0, tiled=True)
    got = got.reshape(out.shape)
    source_band = lax.div(footprint, blocks)
    code = lax.broadcasted_iota(jnp.int32, footprint.shape, 1) * blocks + lax.rem(footprint, blocks)
    here = source_band == band
    low = jnp.min(jnp.where(here, code, blocks * blocks), axis=1)
    high = jnp.max(jnp.where(here, code, -1), axis=1)
    add_index = jnp.stack(
        [
            jnp.where(high >= 0, low & (blocks - 1), blocks),
            jnp.where(high > low, high & (blocks - 1), blocks),
        ]
    )
    send_index = (add_index & (blocks - 1)) ^ lax.broadcasted_iota(jnp.int32, add_index.shape, 0)
    my_band = lax.dynamic_index_in_dim(source_band, band, 0, keepdims=False)
    column = jnp.arange(blocks, dtype=jnp.int32)
    same = (my_band[:, None] == my_band[None, :]) & (column[None, :] < column[:, None])
    my_slot = jnp.any(same, axis=1).astype(jnp.int32)
    beam_index = jnp.stack([my_band, my_slot])
    stands = 4 * ((z - (my_band >> 2)) & (bands // 4 - 1)) + ((y - my_band + 1) & 3)
    read_index = 2 * stands + (my_slot ^ (column & 1))
    parts = heights_out(send_index, mine, figure)
    parts = [moved(part, bands, 0, step - 1) for step, part in enumerate(parts)]
    parts = regroup(parts)
    parts = [moved(part, bands, step, 0) for step, part in enumerate(parts)]
    cos, sin = phases(read_index, parts, bands // 2)
    tiles = second_stage(beam_index, mine, got, approach_tiles, focus_tiles, cos, sin, target)
    tiles = lax.all_to_all(tiles, "band", split_axis=0, concat_axis=0, tiled=True)
    own = collect(add_index, tiles, out.shape[0], BF16)
    whole_band = lax.all_to_all(own, "mode", split_axis=0, concat_axis=0, tiled=True)
    return whole_band.reshape(figure.shape).astype(F32)


def solution(mesh):
    in_specs = (P("mode", "band", None, None), P("band", None), P("band", None), P(), P(), P())
    out_specs = P("band", None)
    return jax.shard_map(shards, mesh=mesh, in_specs=in_specs, out_specs=out_specs, check_vma=False)
```

```python
import functools

import jax
import jax.numpy as jnp
from jax import lax
from jax.experimental import pallas as pl
from jax.experimental.pallas import tpu as pltpu
from jax.sharding import PartitionSpec as P

TILE = 128
HALF = 64
MIRROR_TILE = 64
PHASE_FACTOR = 4.0
F32 = jnp.float32
BF16 = jnp.bfloat16


def whole(*_):
    return pl.BlockSpec(memory_space=pltpu.VMEM)


def write_weights(tiles_ref, w_ref, split):
    for o in range(3):
        re = tiles_ref[o, 0].astype(F32)
        im = tiles_ref[o, 1].astype(F32)
        upper = jnp.concatenate([re, im], axis=1).astype(BF16)
        lower = jnp.concatenate([-im, re], axis=1).astype(BF16)
        if split:
            w_ref[o, 0:64] = upper[0:64]
            w_ref[o, 64:128] = lower[0:64]
            w_ref[o, 128:192] = upper[64:128]
            w_ref[o, 192:256] = lower[64:128]
        else:
            w_ref[o, 0:128] = upper
            w_ref[o, 128:256] = lower


def banded_rows(x_ref, w_ref, row, count, rows, flip=False):
    total = None
    for o in range(3):
        x = x_ref[pl.ds(pl.multiple_of(row + o * rows, 64), count)]
        if flip:
            part = lax.dot_general(x, w_ref[2 - o], (((1,), (1,)), ((), ())), preferred_element_type=F32)
        else:
            part = jnp.dot(x, w_ref[o], preferred_element_type=F32)
        total = part if total is None else total + part
    return total


def first_kernel(field_ref, tiles_ref, out_ref, field_buf, out_buf, wide_ref, x_ref, w_ref, in_sem, out_sem):
    count_tiles = field_ref.shape[0] // 128
    rows = 64
    pitch = 2 * count_tiles + 1
    parts = 4
    lines = rows // parts
    size = lines * 2 * count_tiles
    loads = [
        pltpu.make_async_copy(
            field_ref.at[pl.ds(i * size, size)], field_buf.at[pl.ds(i * size, size)], in_sem.at[i]
        )
        for i in range(parts)
    ]
    for load in loads:
        load.start()
    write_weights(tiles_ref, w_ref, False)
    x_ref[0:rows] = jnp.zeros((rows, 256), BF16)
    x_ref[(count_tiles + 1) * rows : (count_tiles + 2) * rows] = jnp.zeros((rows, 256), BF16)
    for u in range(rows):
        if u % lines == 0:
            loads[u // lines].wait()
        wide_ref[u * pitch : u * pitch + 2 * count_tiles] = field_buf[
            u * 2 * count_tiles : (u + 1) * 2 * count_tiles
        ].astype(F32)
    for j in range(count_tiles):
        for c in range(2):
            x_ref[(j + 1) * rows : (j + 2) * rows, c * 128 : (c + 1) * 128] = wide_ref[
                pl.ds(2 * j + c, rows, stride=pitch)
            ].astype(BF16)
    step = 16
    stores = []
    for q in range(count_tiles // step):
        got = banded_rows(x_ref, w_ref, q * (step * rows), step * rows, rows)
        for t in range(step):
            mine = got[t * rows : (t + 1) * rows]
            stacked = jnp.concatenate([mine[:, 0:128], mine[:, 128:256]], axis=0)
            turned = jnp.transpose(stacked).astype(BF16)
            at = (q * step + t) * 2
            for h in range(2):
                out_buf[:, at + h : at + h + 1] = turned[h * 64 : (h + 1) * 64].reshape(8, 1, 8, 128)
        span = pl.ds(q * 2 * step, 2 * step)
        store = pltpu.make_async_copy(out_buf.at[:, span], out_ref.at[:, span], out_sem.at[q])
        store.start()
        stores.append(store)
    for store in stores:
        store.wait()


def first_stage(field, tiles):
    rows, length = field.shape[1], field.shape[3]
    count = length // TILE
    field = field.reshape(rows, 2, count, TILE).transpose(0, 2, 1, 3).reshape(rows * count * 2, TILE)
    shape = (8, length // 64, 8, 128)
    return pl.pallas_call(
        first_kernel,
        out_shape=jax.ShapeDtypeStruct(shape, BF16),
        in_specs=[pl.BlockSpec(memory_space=pl.ANY), whole()],
        out_specs=pl.BlockSpec(memory_space=pl.ANY),
        scratch_shapes=[
            pltpu.VMEM(field.shape, BF16),
            pltpu.VMEM(shape, BF16),
            pltpu.VMEM((rows * (2 * count + 1), 128), F32),
            pltpu.VMEM(((count + 2) * rows, 256), BF16),
            pltpu.VMEM((3, 256, 256), BF16),
            pltpu.SemaphoreType.DMA((4,)),
            pltpu.SemaphoreType.DMA((count // 16,)),
        ],
        cost_estimate=pl.CostEstimate(flops=2 * rows * count * 768 * 256, bytes_accessed=1 << 21, transcendentals=0),
        name="first",
    )(field, tiles)


def both_ways(wide_ref, at, x):
    wide_ref[2 * at] = x
    wide_ref[2 * at + 1] = pltpu.roll(x, 64, 1)


def heights_out_kernel(mine_ref, footprint_ref, figure_ref, out_ref, rows_ref, tiles_ref):
    bands, blocks = footprint_ref.shape
    pairs = figure_ref.shape[1] // 128
    for p in range(pairs):
        x = figure_ref[:, p * 128 : (p + 1) * 128].astype(F32)
        rows_ref[pl.ds(2 * p * 9, 8)] = x
        rows_ref[pl.ds((2 * p + 1) * 9, 8)] = pltpu.roll(x, 64, 1)
    for r in range(8):
        tiles_ref[:, r * 128 : (r + 1) * 128] = rows_ref[pl.ds(r, blocks, stride=9)].astype(BF16)
    footprint = footprint_ref[...]
    column = lax.broadcasted_iota(jnp.int32, (bands, blocks), 1)
    code = (column * blocks + (footprint & (blocks - 1))).astype(F32)
    here = (footprint >> (blocks.bit_length() - 1)) == mine_ref[1]
    low = jnp.min(jnp.where(here, code, float(blocks * blocks)), axis=1, keepdims=True).astype(jnp.int32)
    high = jnp.max(jnp.where(here, code, 0.0), axis=1, keepdims=True).astype(jnp.int32)
    picked = []
    for c, chosen in enumerate((low, high)):
        hot = column == ((chosen & (blocks - 1)) ^ c)
        hot = jnp.where(hot, 1.0, 0.0).astype(BF16)
        picked.append(jnp.dot(hot, tiles_ref[...], preferred_element_type=F32))
    lane = lax.broadcasted_iota(jnp.int32, (bands, 128), 1)
    for r in range(8):
        at = slice(r * 128, (r + 1) * 128)
        rows_ref[pl.ds(r, bands, stride=9)] = jnp.where(lane < 64, picked[0][:, at], picked[1][:, at])
    for d in range(bands):
        out_ref[d] = rows_ref[pl.ds(9 * d, 8)].astype(BF16)


def heights_out(mine, footprint, figure):
    bands = footprint.shape[0]
    return pl.pallas_call(
        heights_out_kernel,
        out_shape=jax.ShapeDtypeStruct((bands, 8, 128), BF16),
        grid_spec=pltpu.PrefetchScalarGridSpec(
            num_scalar_prefetch=1,
            grid=(1,),
            in_specs=[
                pl.BlockSpec(footprint.shape, lambda g, mine: (0, 0)),
                pl.BlockSpec((8, figure.shape[1]), lambda g, mine: (mine[0], 0)),
            ],
            out_specs=pl.BlockSpec((bands, 8, 128), lambda g, mine: (0, 0, 0)),
            scratch_shapes=[
                pltpu.VMEM((bands * 9, 128), F32),
                pltpu.VMEM((figure.shape[1] // 64, 8 * 128), BF16),
            ],
        ),
        name="heights_out",
    )(mine, footprint, figure)


def phase_kernel(index_ref, tiles_ref, cos_ref, sin_ref, wide_ref):
    lane = lax.broadcasted_iota(jnp.int32, (8, 128), 1)
    pairs = cos_ref.shape[0]
    for s in range(tiles_ref.shape[0]):
        both_ways(wide_ref, s, tiles_ref[s].astype(F32))

    def pair(p, carry):
        phase = PHASE_FACTOR * jnp.where(lane < 64, wide_ref[index_ref[2 * p]], wide_ref[index_ref[2 * p + 1]])
        cos_ref[p] = jnp.cos(phase)
        sin_ref[p] = jnp.sin(phase)
        return carry

    lax.fori_loop(0, pairs, pair, 0, unroll=4)


def phases(index, tiles):
    bands = tiles.shape[0]
    return pl.pallas_call(
        phase_kernel,
        out_shape=[jax.ShapeDtypeStruct((bands // 2, 8, 128), F32)] * 2,
        in_specs=[pl.BlockSpec(memory_space=pltpu.SMEM), whole()],
        out_specs=[whole(), whole()],
        scratch_shapes=[pltpu.VMEM((2 * bands, 8, 128), F32)],
        compiler_params=pltpu.CompilerParams(vmem_limit_bytes=8 << 20),
        name="phases",
    )(index, tiles)


def second_kernel(index_ref, mine_ref, given_ref, approach_ref, focus_ref, cos_ref, sin_ref, target_ref, out_ref,
                  got_ref, x_ref, y_ref, g_ref, wp_ref, wf_ref, sem):
    pairs = cos_ref.shape[0]
    rows = 64
    parts = 4
    size = 2 * pairs // parts
    loads = [
        pltpu.make_async_copy(
            given_ref.at[:, pl.ds(i * size, size)], got_ref.at[:, pl.ds(i * size, size)], sem.at[i]
        )
        for i in range(parts)
    ]
    for load in loads:
        load.start()
    write_weights(approach_ref, wp_ref, True)
    write_weights(focus_ref, wf_ref, False)
    blank = jnp.zeros((rows, 256), BF16)
    for ref in (x_ref, y_ref, g_ref):
        ref[0:rows] = blank
        ref[(pairs + 1) * rows : (pairs + 2) * rows] = blank

    def fill(p, carry):
        to = pl.ds(pl.multiple_of((p + 1) * rows, 64), rows)
        for h in range(2):
            x = got_ref[:, 2 * p + h].astype(F32).reshape(rows, 128)
            x_ref[to, h * 128 : (h + 1) * 128] = x.astype(BF16)
        return carry

    for i in range(parts):
        loads[i].wait()
        lax.fori_loop(i * pairs // parts, (i + 1) * pairs // parts, fill, 0, unroll=4)
    step = 16

    def mirror(q, carry):
        row = q * (step * rows)
        a2 = banded_rows(x_ref, wp_ref, row, step * rows, rows).astype(BF16).astype(F32)
        re = a2[:, 0:128].reshape(step, 8, 8, 128)
        im = a2[:, 128:256].reshape(step, 8, 8, 128)
        cos = cos_ref[pl.ds(q * step, step)][:, None]
        sin = sin_ref[pl.ds(q * step, step)][:, None]
        to = pl.ds(pl.multiple_of(row + rows, 64), step * rows)
        y_ref[to, 0:128] = (re * cos - im * sin).reshape(step * rows, 128).astype(BF16)
        y_ref[to, 128:256] = (re * sin + im * cos).reshape(step * rows, 128).astype(BF16)
        return carry

    lax.fori_loop(0, pairs // step, mirror, 0)

    def detect(q, carry):
        row = q * (step * rows)
        a4 = banded_rows(y_ref, wf_ref, row, step * rows, rows)
        re = a4[:, 0:128].reshape(step, 8, 8, 128)
        im = a4[:, 128:256].reshape(step, 8, 8, 128)
        power = jnp.sum(re * re + im * im, axis=1)
        to = pl.ds(pl.multiple_of(row + rows, 64), step * rows)
        for t in range(step):
            at = pl.ds(pl.multiple_of((q * step + t) * 128, 128), 128)
            left = (power[t] - target_ref[:, at].astype(F32))[None]
            to = pl.ds(pl.multiple_of(row + rows + t * rows, 64), rows)
            g_ref[to, 0:128] = (re[t] * left).reshape(rows, 128).astype(BF16)
            g_ref[to, 128:256] = (im[t] * left).reshape(rows, 128).astype(BF16)
        return carry

    lax.fori_loop(0, pairs // step, detect, 0)
    lane = lax.broadcasted_iota(jnp.int32, (8, 128), 1)
    out_ref[...] = jnp.zeros_like(out_ref)

    def adjoint(q, carry):
        row = q * (step * rows)
        g3 = banded_rows(g_ref, wf_ref, row, step * rows, rows, flip=True)
        own = pl.ds(pl.multiple_of(row + rows, 64), step * rows)
        re = y_ref[own, 0:128].astype(F32)
        im = y_ref[own, 128:256].astype(F32)
        terms = g3[:, 128:256] * re - g3[:, 0:128] * im
        sens = 2.0 * PHASE_FACTOR * jnp.sum(terms.reshape(step, 8, 8, 128), axis=1)
        for t in range(step):
            turned = pltpu.roll(sens[t], 64, 1)
            for h in range(2):
                j = (q * step + t) * 2 + h
                s, c = index_ref[0, j], index_ref[1, j]
                tile = jnp.where(c != h, turned, sens[t])
                out_ref[s] = jnp.where((lane < 64) == (c == 0), tile, out_ref[s].astype(F32)).astype(BF16)
        return carry

    lax.fori_loop(0, pairs // step, adjoint, 0)


def second_stage(index, mine, got, approach, focus, cos, sin, target):
    bands = got.shape[1]
    pairs = bands // 2
    keep = lambda *shape: pl.BlockSpec(shape, lambda g, index, mine: (0,) * len(shape))
    return pl.pallas_call(
        second_kernel,
        out_shape=jax.ShapeDtypeStruct((bands, 8, 128), BF16),
        grid_spec=pltpu.PrefetchScalarGridSpec(
            num_scalar_prefetch=2,
            grid=(1,),
            in_specs=[
                pl.BlockSpec(memory_space=pl.ANY),
                keep(*approach.shape),
                keep(*focus.shape),
                keep(*cos.shape),
                keep(*sin.shape),
                pl.BlockSpec((8, target.shape[1]), lambda g, index, mine: (mine[0], 0)),
            ],
            out_specs=keep(bands, 8, 128),
            scratch_shapes=[pltpu.VMEM(got.shape, BF16)]
            + [pltpu.VMEM(((pairs + 2) * 64, 256), BF16)] * 3
            + [pltpu.VMEM((3, 256, 256), BF16)] * 2
            + [pltpu.SemaphoreType.DMA((4,))],
        ),
        cost_estimate=pl.CostEstimate(flops=6 * 64 * pairs * 768 * 256, bytes_accessed=1 << 20, transcendentals=0),
        compiler_params=pltpu.CompilerParams(vmem_limit_bytes=24 << 20),
        name="second",
    )(index, mine, got, approach, focus, cos, sin, target)


def collect_kernel(index_ref, given_ref, out_ref, tiles_ref, wide_ref, sem, *sums):
    lane = lax.broadcasted_iota(jnp.int32, (8, 128), 1)
    pairs = out_ref.shape[1] // 128
    bands = tiles_ref.shape[0]
    load = pltpu.make_async_copy(given_ref, tiles_ref, sem)
    load.start()
    for part in sums:
        part[...] = jnp.zeros_like(part)
    load.wait()
    for d in range(bands):
        both_ways(wide_ref, d, tiles_ref[d].astype(F32))
    for d in range(bands):
        for c in range(2):
            part = sums[2 * (d % 2) + c]
            k = index_ref[c, d]
            part[k] += wide_ref[2 * d + ((k & 1) ^ c)]
    for p in range(pairs):
        low = sums[0][2 * p] + sums[1][2 * p] + sums[2][2 * p] + sums[3][2 * p]
        high = sums[0][2 * p + 1] + sums[1][2 * p + 1] + sums[2][2 * p + 1] + sums[3][2 * p + 1]
        out_ref[:, p * 128 : (p + 1) * 128] = jnp.where(lane < 64, low, high).astype(out_ref.dtype)


def collect(index, tiles, dtype):
    bands = tiles.shape[0]
    return pl.pallas_call(
        collect_kernel,
        out_shape=jax.ShapeDtypeStruct((8, bands * 64), dtype),
        in_specs=[pl.BlockSpec(memory_space=pltpu.SMEM), pl.BlockSpec(memory_space=pl.ANY)],
        out_specs=whole(),
        scratch_shapes=[
            pltpu.VMEM(tiles.shape, BF16),
            pltpu.VMEM((2 * bands, 8, 128), F32),
            pltpu.SemaphoreType.DMA,
        ]
        + [pltpu.VMEM((bands + 8, 8, 128), F32)] * 4,
        compiler_params=pltpu.CompilerParams(vmem_limit_bytes=8 << 20),
        name="collect",
    )(index, tiles)


def shards(mode_field, figure, target, footprint, approach_tiles, focus_tiles):
    band = lax.axis_index("band").astype(jnp.int32)
    mine = jnp.stack([lax.axis_index("mode").astype(jnp.int32), band])
    blocks = footprint.shape[1]
    heights = heights_out(mine, footprint, figure)
    heights = lax.all_to_all(heights, "band", split_axis=0, concat_axis=0, tiled=True)
    out = first_stage(mode_field, approach_tiles)
    got = lax.all_to_all(out.reshape(-1, 8, 128), ("mode", "band"), split_axis=0, concat_axis=0, tiled=True)
    got = got.reshape(out.shape)
    source_band = lax.div(footprint, blocks)
    code = lax.broadcasted_iota(jnp.int32, footprint.shape, 1) * blocks + lax.rem(footprint, blocks)
    here = source_band == band
    low = jnp.min(jnp.where(here, code, blocks * blocks), axis=1)
    high = jnp.max(jnp.where(here, code, -1), axis=1)
    add_index = jnp.stack(
        [
            jnp.where(high >= 0, low & (blocks - 1), blocks),
            jnp.where(high > low, high & (blocks - 1), blocks),
        ]
    )
    my_band = lax.dynamic_index_in_dim(source_band, band, 0, keepdims=False)
    column = jnp.arange(blocks, dtype=jnp.int32)
    same = (my_band[:, None] == my_band[None, :]) & (column[None, :] < column[:, None])
    my_slot = jnp.any(same, axis=1).astype(jnp.int32)
    cos, sin = phases(2 * my_band + (my_slot ^ (column & 1)), heights)
    beam_index = jnp.stack([my_band, my_slot])
    tiles = second_stage(beam_index, mine, got, approach_tiles, focus_tiles, cos, sin, target)
    tiles = lax.all_to_all(tiles, "band", split_axis=0, concat_axis=0, tiled=True)
    own = collect(add_index, tiles, BF16)
    return lax.all_gather(own, "mode", axis=0, tiled=True).astype(F32)


def solution(mesh):
    in_specs = (P("mode", "band", None, None), P("band", None), P("band", None), P(), P(), P())
    out_specs = P("band", None)
    return jax.shard_map(shards, mesh=mesh, in_specs=in_specs, out_specs=out_specs, check_vma=False)
```

```python
import functools

import jax
import jax.numpy as jnp
from jax import lax
from jax.experimental import pallas as pl
from jax.experimental.pallas import tpu as pltpu
from jax.sharding import PartitionSpec as P

TILE = 128
HALF = 64
MIRROR_TILE = 64
PHASE_FACTOR = 4.0
F32 = jnp.float32
BF16 = jnp.bfloat16


def whole(*_):
    return pl.BlockSpec(memory_space=pltpu.VMEM)


def write_weights(tiles_ref, w_ref, split):
    for o in range(3):
        re = tiles_ref[o, 0].astype(F32)
        im = tiles_ref[o, 1].astype(F32)
        upper = jnp.concatenate([re, im], axis=1).astype(BF16)
        lower = jnp.concatenate([-im, re], axis=1).astype(BF16)
        if split:
            w_ref[o, 0:64] = upper[0:64]
            w_ref[o, 64:128] = lower[0:64]
            w_ref[o, 128:192] = upper[64:128]
            w_ref[o, 192:256] = lower[64:128]
        else:
            w_ref[o, 0:128] = upper
            w_ref[o, 128:256] = lower


def banded_rows(x_ref, w_ref, row, count, rows, flip=False):
    total = None
    for o in range(3):
        x = x_ref[pl.ds(pl.multiple_of(row + o * rows, 64), count)]
        if flip:
            part = lax.dot_general(x, w_ref[2 - o], (((1,), (1,)), ((), ())), preferred_element_type=F32)
        else:
            part = jnp.dot(x, w_ref[o], preferred_element_type=F32)
        total = part if total is None else total + part
    return total


def first_kernel(field_ref, tiles_ref, footprint_ref, figure_ref, out_ref, field_buf, figure_buf, out_buf, wide_ref,
                 spread_ref, rows_ref, pick_ref, chunk_ref, x_ref, w_ref, in_sem, out_sem):
    count_tiles = field_ref.shape[0] // 128
    bands, blocks = footprint_ref.shape
    rows = 64
    pitch = 2 * count_tiles + 1
    parts = 4
    lines = rows // parts
    size = lines * 2 * count_tiles
    figure_load = pltpu.make_async_copy(figure_ref, figure_buf, in_sem.at[parts])
    figure_load.start()
    loads = [
        pltpu.make_async_copy(
            field_ref.at[pl.ds(i * size, size)], field_buf.at[pl.ds(i * size, size)], in_sem.at[i]
        )
        for i in range(parts)
    ]
    for load in loads:
        load.start()
    write_weights(tiles_ref, w_ref, False)
    x_ref[0:rows] = jnp.zeros((rows, 256), BF16)
    x_ref[(count_tiles + 1) * rows : (count_tiles + 2) * rows] = jnp.zeros((rows, 256), BF16)
    chunk_ref[pl.ds(9, 8 * bands, stride=10)] = jnp.zeros((8 * bands, 128), F32)

    mode, band = lax.axis_index("mode"), lax.axis_index("band")
    figure_load.wait()
    for p in range(blocks // 2):
        x = figure_buf[:, p * 128 : (p + 1) * 128].astype(F32)
        for g in range(8):
            spread_ref[pl.ds(p * 72 + g * 9, 8)] = x[g * 8 : (g + 1) * 8]
        mine = spread_ref[pl.ds(p * 72 + mode, 8, stride=9)]
        rows_ref[pl.ds(2 * p * 9, 8)] = mine
        rows_ref[pl.ds((2 * p + 1) * 9, 8)] = pltpu.roll(mine, 64, 1)
    for i in range(8):
        pick_ref[:, i * 128 : (i + 1) * 128] = rows_ref[pl.ds(i, blocks, stride=9)].astype(BF16)
    footprint = footprint_ref[...]
    column = lax.broadcasted_iota(jnp.int32, (bands, blocks), 1)
    code = (column * blocks + (footprint & (blocks - 1))).astype(F32)
    here = (footprint >> (blocks.bit_length() - 1)) == band
    low = jnp.min(jnp.where(here, code, float(blocks * blocks)), axis=1, keepdims=True).astype(jnp.int32)
    high = jnp.max(jnp.where(here, code, 0.0), axis=1, keepdims=True).astype(jnp.int32)
    picked = []
    for c, chosen in enumerate((low, high)):
        hot = column == ((chosen & (blocks - 1)) ^ c)
        hot = jnp.where(hot, 1.0, 0.0).astype(BF16)
        picked.append(jnp.dot(hot, pick_ref[...], preferred_element_type=F32))
    lane = lax.broadcasted_iota(jnp.int32, (bands, 128), 1)
    for i in range(8):
        at = slice(i * 128, (i + 1) * 128)
        chunk_ref[pl.ds(i * bands * 10 + 8, bands, stride=10)] = jnp.where(lane < 64, picked[0][:, at], picked[1][:, at])

    for u in range(rows):
        if u % lines == 0:
            loads[u // lines].wait()
        wide_ref[u * pitch : u * pitch + 2 * count_tiles] = field_buf[
            u * 2 * count_tiles : (u + 1) * 2 * count_tiles
        ].astype(F32)
    for j in range(count_tiles):
        for c in range(2):
            x_ref[(j + 1) * rows : (j + 2) * rows, c * 128 : (c + 1) * 128] = wide_ref[
                pl.ds(2 * j + c, rows, stride=pitch)
            ].astype(BF16)
    step = 16
    stores = []
    for q in range(count_tiles // step):
        got = banded_rows(x_ref, w_ref, q * (step * rows), step * rows, rows)
        for t in range(step):
            mine = got[t * rows : (t + 1) * rows]
            stacked = jnp.concatenate([mine[:, 0:128], mine[:, 128:256]], axis=0)
            turned = jnp.transpose(stacked)
            at = (q * step + t) * 2
            for h in range(2):
                for i in range(8):
                    from_row = h * 64 + i * 8
                    chunk_ref[pl.ds((i * bands + at + h) * 10, 8)] = turned[from_row : from_row + 8]
        span = 2 * step * 10
        for i in range(8):
            at = i * bands * 10 + q * span
            out_buf[at : at + span] = chunk_ref[at : at + span].astype(BF16)
            store = pltpu.make_async_copy(
                out_buf.at[pl.ds(at, span)], out_ref.at[pl.ds(at, span)], out_sem.at[q * 8 + i]
            )
            store.start()
            stores.append(store)
    for store in stores:
        store.wait()


def first_stage(field, tiles, footprint, figure):
    rows, length = field.shape[1], field.shape[3]
    count = length // TILE
    bands, blocks = footprint.shape
    field = field.reshape(rows, 2, count, TILE).transpose(0, 2, 1, 3).reshape(rows * count * 2, TILE)
    shape = (8 * bands * 10, TILE)
    return pl.pallas_call(
        first_kernel,
        out_shape=jax.ShapeDtypeStruct(shape, BF16),
        in_specs=[pl.BlockSpec(memory_space=pl.ANY), whole(), whole(), pl.BlockSpec(memory_space=pl.ANY)],
        out_specs=pl.BlockSpec(memory_space=pl.ANY),
        scratch_shapes=[
            pltpu.VMEM(field.shape, BF16),
            pltpu.VMEM(figure.shape, BF16),
            pltpu.VMEM(shape, BF16),
            pltpu.VMEM((rows * (2 * count + 1), 128), F32),
            pltpu.VMEM((blocks // 2 * 72, 128), F32),
            pltpu.VMEM((blocks * 9, 128), F32),
            pltpu.VMEM((blocks, 8 * 128), BF16),
            pltpu.VMEM(shape, F32),
            pltpu.VMEM(((count + 2) * rows, 256), BF16),
            pltpu.VMEM((3, 256, 256), BF16),
            pltpu.SemaphoreType.DMA((5,)),
            pltpu.SemaphoreType.DMA((8 * (count // 16),)),
        ],
        cost_estimate=pl.CostEstimate(flops=2 * rows * count * 768 * 256, bytes_accessed=1 << 21, transcendentals=0),
        name="first",
    )(field, tiles, footprint, figure)


def both_ways(wide_ref, at, x):
    wide_ref[2 * at] = x
    wide_ref[2 * at + 1] = pltpu.roll(x, 64, 1)


def second_kernel(index_ref, given_ref, approach_ref, focus_ref, target_ref, out_ref,
                  got_ref, wide_ref, heights_ref, cos_ref, sin_ref, want_ref, x_ref, y_ref, g_ref, wp_ref, wf_ref, sem):
    pairs = cos_ref.shape[0]
    bands = 2 * pairs
    rows = 64
    parts = 4
    size = given_ref.shape[0] // parts
    loads = [
        pltpu.make_async_copy(given_ref.at[pl.ds(i * size, size)], got_ref.at[pl.ds(i * size, size)], sem.at[i])
        for i in range(parts)
    ]
    mode = lax.axis_index("mode")
    loads.append(
        pltpu.make_async_copy(target_ref.at[pl.ds(pl.multiple_of(mode * 8, 8), 8)], want_ref, sem.at[parts])
    )
    for load in loads:
        load.start()
    write_weights(approach_ref, wp_ref, True)
    write_weights(focus_ref, wf_ref, False)
    blank = jnp.zeros((rows, 256), BF16)
    for ref in (x_ref, y_ref, g_ref):
        ref[0:rows] = blank
        ref[(pairs + 1) * rows : (pairs + 2) * rows] = blank
    for i in range(parts):
        loads[i].wait()
        wide_ref[i * size : (i + 1) * size] = got_ref[i * size : (i + 1) * size].astype(F32)
    loads[parts].wait()

    for p in range(pairs):
        for h in range(2):
            x = [wide_ref[pl.ds((m * bands + 2 * p + h) * 10, 8)] for m in range(8)]
            x_ref[(p + 1) * rows : (p + 2) * rows, h * 128 : (h + 1) * 128] = jnp.concatenate(x, axis=0).astype(BF16)
    for s in range(bands):
        both_ways(heights_ref, s, wide_ref[pl.ds(s * 10 + 8, 8, stride=bands * 10)])
    lane = lax.broadcasted_iota(jnp.int32, (8, 128), 1)

    def mirror_pair(p, carry):
        a, b = heights_ref[index_ref[2, 2 * p]], heights_ref[index_ref[2, 2 * p + 1]]
        phase = PHASE_FACTOR * jnp.where(lane < 64, a, b)
        cos_ref[p] = jnp.cos(phase)
        sin_ref[p] = jnp.sin(phase)
        return carry

    lax.fori_loop(0, pairs, mirror_pair, 0, unroll=4)
    step = 16

    def mirror(q, carry):
        row = q * (step * rows)
        a2 = banded_rows(x_ref, wp_ref, row, step * rows, rows).astype(BF16).astype(F32)
        re = a2[:, 0:128].reshape(step, 8, 8, 128)
        im = a2[:, 128:256].reshape(step, 8, 8, 128)
        cos = cos_ref[pl.ds(q * step, step)][:, None]
        sin = sin_ref[pl.ds(q * step, step)][:, None]
        to = pl.ds(pl.multiple_of(row + rows, 64), step * rows)
        y_ref[to, 0:128] = (re * cos - im * sin).reshape(step * rows, 128).astype(BF16)
        y_ref[to, 128:256] = (re * sin + im * cos).reshape(step * rows, 128).astype(BF16)
        return carry

    lax.fori_loop(0, pairs // step, mirror, 0)

    def detect(q, carry):
        row = q * (step * rows)
        a4 = banded_rows(y_ref, wf_ref, row, step * rows, rows)
        re = a4[:, 0:128].reshape(step, 8, 8, 128)
        im = a4[:, 128:256].reshape(step, 8, 8, 128)
        power = jnp.sum(re * re + im * im, axis=1)
        to = pl.ds(pl.multiple_of(row + rows, 64), step * rows)
        for t in range(step):
            at = pl.ds(pl.multiple_of((q * step + t) * 128, 128), 128)
            left = (power[t] - want_ref[:, at].astype(F32))[None]
            to = pl.ds(pl.multiple_of(row + rows + t * rows, 64), rows)
            g_ref[to, 0:128] = (re[t] * left).reshape(rows, 128).astype(BF16)
            g_ref[to, 128:256] = (im[t] * left).reshape(rows, 128).astype(BF16)
        return carry

    lax.fori_loop(0, pairs // step, detect, 0)
    out_ref[...] = jnp.zeros_like(out_ref)

    def adjoint(q, carry):
        row = q * (step * rows)
        g3 = banded_rows(g_ref, wf_ref, row, step * rows, rows, flip=True)
        own = pl.ds(pl.multiple_of(row + rows, 64), step * rows)
        re = y_ref[own, 0:128].astype(F32)
        im = y_ref[own, 128:256].astype(F32)
        terms = g3[:, 128:256] * re - g3[:, 0:128] * im
        sens = 2.0 * PHASE_FACTOR * jnp.sum(terms.reshape(step, 8, 8, 128), axis=1)
        for t in range(step):
            turned = pltpu.roll(sens[t], 64, 1)
            for h in range(2):
                j = (q * step + t) * 2 + h
                s, c = index_ref[0, j], index_ref[1, j]
                tile = jnp.where(c != h, turned, sens[t])
                out_ref[s] = jnp.where((lane < 64) == (c == 0), tile, out_ref[s].astype(F32)).astype(BF16)
        return carry

    lax.fori_loop(0, pairs // step, adjoint, 0)


def second_stage(index, got, approach, focus, target, bands):
    pairs = bands // 2
    anywhere = pl.BlockSpec(memory_space=pl.ANY)
    return pl.pallas_call(
        second_kernel,
        out_shape=jax.ShapeDtypeStruct((bands, 8, 128), BF16),
        in_specs=[pl.BlockSpec(memory_space=pltpu.SMEM), anywhere, whole(), whole(), anywhere],
        out_specs=whole(),
        scratch_shapes=[
            pltpu.VMEM(got.shape, BF16),
            pltpu.VMEM(got.shape, F32),
            pltpu.VMEM((2 * bands, 8, 128), F32),
            pltpu.VMEM((pairs, 8, 128), F32),
            pltpu.VMEM((pairs, 8, 128), F32),
            pltpu.VMEM((8, target.shape[1]), BF16),
        ]
        + [pltpu.VMEM(((pairs + 2) * 64, 256), BF16)] * 3
        + [pltpu.VMEM((3, 256, 256), BF16)] * 2
        + [pltpu.SemaphoreType.DMA((5,))],
        cost_estimate=pl.CostEstimate(flops=6 * 64 * pairs * 768 * 256, bytes_accessed=1 << 20, transcendentals=0),
        compiler_params=pltpu.CompilerParams(vmem_limit_bytes=32 << 20),
        name="second",
    )(index, got, approach, focus, target)


def collect_kernel(index_ref, given_ref, out_ref, tiles_ref, wide_ref, sem, *sums):
    lane = lax.broadcasted_iota(jnp.int32, (8, 128), 1)
    pairs = out_ref.shape[1] // 128
    bands = tiles_ref.shape[0]
    load = pltpu.make_async_copy(given_ref, tiles_ref, sem)
    load.start()
    for part in sums:
        part[...] = jnp.zeros_like(part)
    load.wait()
    for d in range(bands):
        both_ways(wide_ref, d, tiles_ref[d].astype(F32))
    for d in range(bands):
        for c in range(2):
            part = sums[2 * (d % 2) + c]
            k = index_ref[c, d]
            part[k] += wide_ref[2 * d + ((k & 1) ^ c)]
    for p in range(pairs):
        low = sums[0][2 * p] + sums[1][2 * p] + sums[2][2 * p] + sums[3][2 * p]
        high = sums[0][2 * p + 1] + sums[1][2 * p + 1] + sums[2][2 * p + 1] + sums[3][2 * p + 1]
        out_ref[:, p * 128 : (p + 1) * 128] = jnp.where(lane < 64, low, high).astype(out_ref.dtype)


def collect(index, tiles, dtype):
    bands = tiles.shape[0]
    return pl.pallas_call(
        collect_kernel,
        out_shape=jax.ShapeDtypeStruct((8, bands * 64), dtype),
        in_specs=[pl.BlockSpec(memory_space=pltpu.SMEM), pl.BlockSpec(memory_space=pl.ANY)],
        out_specs=whole(),
        scratch_shapes=[
            pltpu.VMEM(tiles.shape, BF16),
            pltpu.VMEM((2 * bands, 8, 128), F32),
            pltpu.SemaphoreType.DMA,
        ]
        + [pltpu.VMEM((bands + 8, 8, 128), F32)] * 4,
        compiler_params=pltpu.CompilerParams(vmem_limit_bytes=8 << 20),
        name="collect",
    )(index, tiles)


def shards(mode_field, figure, target, footprint, approach_tiles, focus_tiles):
    band = lax.axis_index("band").astype(jnp.int32)
    bands, blocks = footprint.shape
    out = first_stage(mode_field, approach_tiles, footprint, figure)
    sent = out.reshape(-1, 5, 2, TILE).transpose(0, 2, 1, 3).reshape(-1, 2, 5 * TILE)
    got = lax.all_to_all(sent, ("mode", "band"), split_axis=0, concat_axis=0, tiled=True)
    got = got.reshape(-1, 2, 5, TILE).transpose(0, 2, 1, 3).reshape(out.shape)
    source_band = lax.div(footprint, blocks)
    code = lax.broadcasted_iota(jnp.int32, footprint.shape, 1) * blocks + lax.rem(footprint, blocks)
    here = source_band == band
    low = jnp.min(jnp.where(here, code, blocks * blocks), axis=1)
    high = jnp.max(jnp.where(here, code, -1), axis=1)
    add_index = jnp.stack(
        [
            jnp.where(high >= 0, low & (blocks - 1), blocks),
            jnp.where(high > low, high & (blocks - 1), blocks),
        ]
    )
    my_band = lax.dynamic_index_in_dim(source_band, band, 0, keepdims=False)
    column = jnp.arange(blocks, dtype=jnp.int32)
    same = (my_band[:, None] == my_band[None, :]) & (column[None, :] < column[:, None])
    my_slot = jnp.any(same, axis=1).astype(jnp.int32)
    beam_index = jnp.stack([my_band, my_slot, 2 * my_band + (my_slot ^ (column & 1))])
    tiles = second_stage(beam_index, got, approach_tiles, focus_tiles, target, bands)
    tiles = lax.all_to_all(tiles, "band", split_axis=0, concat_axis=0, tiled=True)
    own = collect(add_index, tiles, BF16)
    return lax.all_gather(own, "mode", axis=0, tiled=True).astype(F32)


def solution(mesh):
    in_specs = (P("mode", "band", None, None), P("band", None), P("band", None), P(), P(), P())
    out_specs = P("band", None)
    return jax.shard_map(shards, mesh=mesh, in_specs=in_specs, out_specs=out_specs, check_vma=False)
```

```python
import functools

import jax
import jax.numpy as jnp
from jax import lax
from jax.experimental import pallas as pl
from jax.experimental.pallas import tpu as pltpu
from jax.sharding import PartitionSpec as P

TILE = 128
HALF = 64
MIRROR_TILE = 64
PHASE_FACTOR = 4.0
F32 = jnp.float32
BF16 = jnp.bfloat16


def place(mode, band, modes, bands):
    return (mode + modes // 2) % modes * bands + (band + bands // 2) % bands


def whole(*_):
    return pl.BlockSpec(memory_space=pltpu.VMEM)


def write_weights(tiles_ref, w_ref, split):
    for o in range(3):
        re = tiles_ref[o, 0].astype(F32)
        im = tiles_ref[o, 1].astype(F32)
        upper = jnp.concatenate([re, im], axis=1).astype(BF16)
        lower = jnp.concatenate([-im, re], axis=1).astype(BF16)
        if split:
            w_ref[o, 0:64] = upper[0:64]
            w_ref[o, 64:128] = lower[0:64]
            w_ref[o, 128:192] = upper[64:128]
            w_ref[o, 192:256] = lower[64:128]
        else:
            w_ref[o, 0:128] = upper
            w_ref[o, 128:256] = lower


def banded_rows(x_ref, w_ref, row, count, rows, flip=False):
    total = None
    for o in range(3):
        x = x_ref[pl.ds(pl.multiple_of(row + o * rows, 64), count)]
        if flip:
            part = lax.dot_general(x, w_ref[2 - o], (((1,), (1,)), ((), ())), preferred_element_type=F32)
        else:
            part = jnp.dot(x, w_ref[o], preferred_element_type=F32)
        total = part if total is None else total + part
    return total


def first_kernel(field_ref, tiles_ref, footprint_ref, figure_ref, out_ref, field_buf, figure_buf, out_buf, wide_ref,
                 spread_ref, rows_ref, pick_ref, chunk_ref, x_ref, w_ref, in_sem, out_sem):
    count_tiles = field_ref.shape[0] // 128
    bands, blocks = footprint_ref.shape
    rows = 64
    pitch = 2 * count_tiles + 1
    parts = 4
    lines = rows // parts
    size = lines * 2 * count_tiles
    figure_load = pltpu.make_async_copy(figure_ref, figure_buf, in_sem.at[parts])
    figure_load.start()
    loads = [
        pltpu.make_async_copy(
            field_ref.at[pl.ds(i * size, size)], field_buf.at[pl.ds(i * size, size)], in_sem.at[i]
        )
        for i in range(parts)
    ]
    for load in loads:
        load.start()
    write_weights(tiles_ref, w_ref, False)
    x_ref[0:rows] = jnp.zeros((rows, 256), BF16)
    x_ref[(count_tiles + 1) * rows : (count_tiles + 2) * rows] = jnp.zeros((rows, 256), BF16)
    chunk_ref[pl.ds(9, 8 * bands, stride=10)] = jnp.zeros((8 * bands, 128), F32)

    mode, band = lax.axis_index("mode"), lax.axis_index("band")
    figure_load.wait()
    for p in range(blocks // 2):
        x = figure_buf[:, p * 128 : (p + 1) * 128].astype(F32)
        for g in range(8):
            spread_ref[pl.ds(p * 72 + g * 9, 8)] = x[g * 8 : (g + 1) * 8]
        mine = spread_ref[pl.ds(p * 72 + mode, 8, stride=9)]
        rows_ref[pl.ds(2 * p * 9, 8)] = mine
        rows_ref[pl.ds((2 * p + 1) * 9, 8)] = pltpu.roll(mine, 64, 1)
    for i in range(8):
        pick_ref[:, i * 128 : (i + 1) * 128] = rows_ref[pl.ds(i, blocks, stride=9)].astype(BF16)
    footprint = footprint_ref[...]
    column = lax.broadcasted_iota(jnp.int32, (bands, blocks), 1)
    code = (column * blocks + (footprint & (blocks - 1))).astype(F32)
    here = (footprint >> (blocks.bit_length() - 1)) == band
    low = jnp.min(jnp.where(here, code, float(blocks * blocks)), axis=1, keepdims=True).astype(jnp.int32)
    high = jnp.max(jnp.where(here, code, 0.0), axis=1, keepdims=True).astype(jnp.int32)
    picked = []
    for c, chosen in enumerate((low, high)):
        hot = column == ((chosen & (blocks - 1)) ^ c)
        hot = jnp.where(hot, 1.0, 0.0).astype(BF16)
        picked.append(jnp.dot(hot, pick_ref[...], preferred_element_type=F32))
    lane = lax.broadcasted_iota(jnp.int32, (bands, 128), 1)
    for i in range(8):
        at = slice(i * 128, (i + 1) * 128)
        mine = jnp.where(lane < 64, picked[0][:, at], picked[1][:, at])
        for part in (0, bands // 2):
            to = place(i, part, 8, bands) * 10 + 8
            chunk_ref[pl.ds(to, bands // 2, stride=10)] = mine[part : part + bands // 2]

    for u in range(rows):
        if u % lines == 0:
            loads[u // lines].wait()
        wide_ref[u * pitch : u * pitch + 2 * count_tiles] = field_buf[
            u * 2 * count_tiles : (u + 1) * 2 * count_tiles
        ].astype(F32)
    for j in range(count_tiles):
        for c in range(2):
            x_ref[(j + 1) * rows : (j + 2) * rows, c * 128 : (c + 1) * 128] = wide_ref[
                pl.ds(2 * j + c, rows, stride=pitch)
            ].astype(BF16)
    step = 16
    stores = []
    for q in range(count_tiles // step):
        got = banded_rows(x_ref, w_ref, q * (step * rows), step * rows, rows)
        for t in range(step):
            mine = got[t * rows : (t + 1) * rows]
            stacked = jnp.concatenate([mine[:, 0:128], mine[:, 128:256]], axis=0)
            turned = jnp.transpose(stacked)
            at = (q * step + t) * 2
            for h in range(2):
                for i in range(8):
                    from_row = h * 64 + i * 8
                    chunk_ref[pl.ds(place(i, at + h, 8, bands) * 10, 8)] = turned[from_row : from_row + 8]
        span = 2 * step * 10
        for i in range(8):
            at = place(i, 2 * step * q, 8, bands) * 10
            out_buf[at : at + span] = chunk_ref[at : at + span].astype(BF16)
            store = pltpu.make_async_copy(
                out_buf.at[pl.ds(at, span)], out_ref.at[pl.ds(at, span)], out_sem.at[q * 8 + i]
            )
            store.start()
            stores.append(store)
    for store in stores:
        store.wait()


def first_stage(field, tiles, footprint, figure):
    rows, length = field.shape[1], field.shape[3]
    count = length // TILE
    bands, blocks = footprint.shape
    field = field.reshape(rows, 2, count, TILE).transpose(0, 2, 1, 3).reshape(rows * count * 2, TILE)
    shape = (8 * bands * 10, TILE)
    return pl.pallas_call(
        first_kernel,
        out_shape=jax.ShapeDtypeStruct(shape, BF16),
        in_specs=[pl.BlockSpec(memory_space=pl.ANY), whole(), whole(), pl.BlockSpec(memory_space=pl.ANY)],
        out_specs=pl.BlockSpec(memory_space=pl.ANY),
        scratch_shapes=[
            pltpu.VMEM(field.shape, BF16),
            pltpu.VMEM(figure.shape, BF16),
            pltpu.VMEM(shape, BF16),
            pltpu.VMEM((rows * (2 * count + 1), 128), F32),
            pltpu.VMEM((blocks // 2 * 72, 128), F32),
            pltpu.VMEM((blocks * 9, 128), F32),
            pltpu.VMEM((blocks, 8 * 128), BF16),
            pltpu.VMEM(shape, F32),
            pltpu.VMEM(((count + 2) * rows, 256), BF16),
            pltpu.VMEM((3, 256, 256), BF16),
            pltpu.SemaphoreType.DMA((5,)),
            pltpu.SemaphoreType.DMA((8 * (count // 16),)),
        ],
        cost_estimate=pl.CostEstimate(flops=2 * rows * count * 768 * 256, bytes_accessed=1 << 21, transcendentals=0),
        name="first",
    )(field, tiles, footprint, figure)


def both_ways(wide_ref, at, x):
    wide_ref[2 * at] = x
    wide_ref[2 * at + 1] = pltpu.roll(x, 64, 1)


def second_kernel(index_ref, given_ref, approach_ref, focus_ref, target_ref, out_ref,
                  got_ref, wide_ref, heights_ref, cos_ref, sin_ref, want_ref, x_ref, y_ref, g_ref, wp_ref, wf_ref, sem):
    pairs = cos_ref.shape[0]
    bands = 2 * pairs
    rows = 64
    parts = 4
    size = given_ref.shape[0] // parts
    loads = [
        pltpu.make_async_copy(given_ref.at[pl.ds(i * size, size)], got_ref.at[pl.ds(i * size, size)], sem.at[i])
        for i in range(parts)
    ]
    mode = lax.axis_index("mode")
    loads.append(
        pltpu.make_async_copy(target_ref.at[pl.ds(pl.multiple_of(mode * 8, 8), 8)], want_ref, sem.at[parts])
    )
    for load in loads:
        load.start()
    write_weights(approach_ref, wp_ref, True)
    write_weights(focus_ref, wf_ref, False)
    blank = jnp.zeros((rows, 256), BF16)
    for ref in (x_ref, y_ref, g_ref):
        ref[0:rows] = blank
        ref[(pairs + 1) * rows : (pairs + 2) * rows] = blank
    for i in range(parts):
        loads[i].wait()
        wide_ref[i * size : (i + 1) * size] = got_ref[i * size : (i + 1) * size].astype(F32)
    loads[parts].wait()

    for p in range(pairs):
        for h in range(2):
            x = [wide_ref[pl.ds(place(m, 2 * p + h, 8, bands) * 10, 8)] for m in range(8)]
            x_ref[(p + 1) * rows : (p + 2) * rows, h * 128 : (h + 1) * 128] = jnp.concatenate(x, axis=0).astype(BF16)
    for s in range(bands):
        x = wide_ref[pl.ds(place(4, s, 8, bands) * 10 + 8, 8, stride=bands * 10)]
        both_ways(heights_ref, s, pltpu.roll(x, 4, 0))
    lane = lax.broadcasted_iota(jnp.int32, (8, 128), 1)

    def mirror_pair(p, carry):
        a, b = heights_ref[index_ref[2, 2 * p]], heights_ref[index_ref[2, 2 * p + 1]]
        phase = PHASE_FACTOR * jnp.where(lane < 64, a, b)
        cos_ref[p] = jnp.cos(phase)
        sin_ref[p] = jnp.sin(phase)
        return carry

    lax.fori_loop(0, pairs, mirror_pair, 0, unroll=4)
    step = 16

    def mirror(q, carry):
        row = q * (step * rows)
        a2 = banded_rows(x_ref, wp_ref, row, step * rows, rows).astype(BF16).astype(F32)
        re = a2[:, 0:128].reshape(step, 8, 8, 128)
        im = a2[:, 128:256].reshape(step, 8, 8, 128)
        cos = cos_ref[pl.ds(q * step, step)][:, None]
        sin = sin_ref[pl.ds(q * step, step)][:, None]
        to = pl.ds(pl.multiple_of(row + rows, 64), step * rows)
        y_ref[to, 0:128] = (re * cos - im * sin).reshape(step * rows, 128).astype(BF16)
        y_ref[to, 128:256] = (re * sin + im * cos).reshape(step * rows, 128).astype(BF16)
        return carry

    lax.fori_loop(0, pairs // step, mirror, 0)

    def detect(q, carry):
        row = q * (step * rows)
        a4 = banded_rows(y_ref, wf_ref, row, step * rows, rows)
        re = a4[:, 0:128].reshape(step, 8, 8, 128)
        im = a4[:, 128:256].reshape(step, 8, 8, 128)
        power = jnp.sum(re * re + im * im, axis=1)
        to = pl.ds(pl.multiple_of(row + rows, 64), step * rows)
        for t in range(step):
            at = pl.ds(pl.multiple_of((q * step + t) * 128, 128), 128)
            left = (power[t] - want_ref[:, at].astype(F32))[None]
            to = pl.ds(pl.multiple_of(row + rows + t * rows, 64), rows)
            g_ref[to, 0:128] = (re[t] * left).reshape(rows, 128).astype(BF16)
            g_ref[to, 128:256] = (im[t] * left).reshape(rows, 128).astype(BF16)
        return carry

    lax.fori_loop(0, pairs // step, detect, 0)
    out_ref[...] = jnp.zeros_like(out_ref)

    def adjoint(q, carry):
        row = q * (step * rows)
        g3 = banded_rows(g_ref, wf_ref, row, step * rows, rows, flip=True)
        own = pl.ds(pl.multiple_of(row + rows, 64), step * rows)
        re = y_ref[own, 0:128].astype(F32)
        im = y_ref[own, 128:256].astype(F32)
        terms = g3[:, 128:256] * re - g3[:, 0:128] * im
        sens = 2.0 * PHASE_FACTOR * jnp.sum(terms.reshape(step, 8, 8, 128), axis=1)
        for t in range(step):
            turned = pltpu.roll(sens[t], 64, 1)
            for h in range(2):
                j = (q * step + t) * 2 + h
                s, c = index_ref[0, j], index_ref[1, j]
                tile = jnp.where(c != h, turned, sens[t])
                out_ref[s] = jnp.where((lane < 64) == (c == 0), tile, out_ref[s].astype(F32)).astype(BF16)
        return carry

    lax.fori_loop(0, pairs // step, adjoint, 0)


def second_stage(index, got, approach, focus, target, bands):
    pairs = bands // 2
    anywhere = pl.BlockSpec(memory_space=pl.ANY)
    return pl.pallas_call(
        second_kernel,
        out_shape=jax.ShapeDtypeStruct((bands, 8, 128), BF16),
        in_specs=[pl.BlockSpec(memory_space=pltpu.SMEM), anywhere, whole(), whole(), anywhere],
        out_specs=whole(),
        scratch_shapes=[
            pltpu.VMEM(got.shape, BF16),
            pltpu.VMEM(got.shape, F32),
            pltpu.VMEM((2 * bands, 8, 128), F32),
            pltpu.VMEM((pairs, 8, 128), F32),
            pltpu.VMEM((pairs, 8, 128), F32),
            pltpu.VMEM((8, target.shape[1]), BF16),
        ]
        + [pltpu.VMEM(((pairs + 2) * 64, 256), BF16)] * 3
        + [pltpu.VMEM((3, 256, 256), BF16)] * 2
        + [pltpu.SemaphoreType.DMA((5,))],
        cost_estimate=pl.CostEstimate(flops=6 * 64 * pairs * 768 * 256, bytes_accessed=1 << 20, transcendentals=0),
        compiler_params=pltpu.CompilerParams(vmem_limit_bytes=32 << 20),
        name="second",
    )(index, got, approach, focus, target)


def collect_kernel(index_ref, given_ref, out_ref, tiles_ref, wide_ref, sem, *sums):
    lane = lax.broadcasted_iota(jnp.int32, (8, 128), 1)
    pairs = out_ref.shape[1] // 128
    bands = tiles_ref.shape[0]
    load = pltpu.make_async_copy(given_ref, tiles_ref, sem)
    load.start()
    for part in sums:
        part[...] = jnp.zeros_like(part)
    load.wait()
    for d in range(bands):
        both_ways(wide_ref, d, tiles_ref[d].astype(F32))
    for d in range(bands):
        for c in range(2):
            part = sums[2 * (d % 2) + c]
            k = index_ref[c, d]
            part[k] += wide_ref[2 * d + ((k & 1) ^ c)]
    for p in range(pairs):
        low = sums[0][2 * p] + sums[1][2 * p] + sums[2][2 * p] + sums[3][2 * p]
        high = sums[0][2 * p + 1] + sums[1][2 * p + 1] + sums[2][2 * p + 1] + sums[3][2 * p + 1]
        out_ref[:, p * 128 : (p + 1) * 128] = jnp.where(lane < 64, low, high).astype(out_ref.dtype)


def collect(index, tiles, dtype):
    bands = tiles.shape[0]
    return pl.pallas_call(
        collect_kernel,
        out_shape=jax.ShapeDtypeStruct((8, bands * 64), dtype),
        in_specs=[pl.BlockSpec(memory_space=pltpu.SMEM), pl.BlockSpec(memory_space=pl.ANY)],
        out_specs=whole(),
        scratch_shapes=[
            pltpu.VMEM(tiles.shape, BF16),
            pltpu.VMEM((2 * bands, 8, 128), F32),
            pltpu.SemaphoreType.DMA,
        ]
        + [pltpu.VMEM((bands + 8, 8, 128), F32)] * 4,
        compiler_params=pltpu.CompilerParams(vmem_limit_bytes=8 << 20),
        name="collect",
    )(index, tiles)


def shards(mode_field, figure, target, footprint, approach_tiles, focus_tiles):
    band = lax.axis_index("band").astype(jnp.int32)
    bands, blocks = footprint.shape
    out = first_stage(mode_field, approach_tiles, footprint, figure)
    sent = out.reshape(-1, 5, 2, TILE).transpose(0, 2, 1, 3).reshape(-1, 2, 5 * TILE)
    order = sorted(range(8 * bands), key=lambda k: place(k // bands, k % bands, 8, bands))
    got = lax.all_to_all(sent, ("mode", "band"), split_axis=0, concat_axis=0, tiled=True, axis_index_groups=[order])
    got = got.reshape(-1, 2, 5, TILE).transpose(0, 2, 1, 3).reshape(out.shape)
    source_band = lax.div(footprint, blocks)
    code = lax.broadcasted_iota(jnp.int32, footprint.shape, 1) * blocks + lax.rem(footprint, blocks)
    here = source_band == band
    low = jnp.min(jnp.where(here, code, blocks * blocks), axis=1)
    high = jnp.max(jnp.where(here, code, -1), axis=1)
    add_index = jnp.stack(
        [
            jnp.where(high >= 0, low & (blocks - 1), blocks),
            jnp.where(high > low, high & (blocks - 1), blocks),
        ]
    )
    my_band = lax.dynamic_index_in_dim(source_band, band, 0, keepdims=False)
    column = jnp.arange(blocks, dtype=jnp.int32)
    same = (my_band[:, None] == my_band[None, :]) & (column[None, :] < column[:, None])
    my_slot = jnp.any(same, axis=1).astype(jnp.int32)
    beam_index = jnp.stack([my_band, my_slot, 2 * my_band + (my_slot ^ (column & 1))])
    tiles = second_stage(beam_index, got, approach_tiles, focus_tiles, target, bands)
    tiles = lax.all_to_all(tiles, "band", split_axis=0, concat_axis=0, tiled=True)
    own = collect(add_index, tiles, BF16)
    return lax.all_gather(own, "mode", axis=0, tiled=True).astype(F32)


def solution(mesh):
    in_specs = (P("mode", "band", None, None), P("band", None), P("band", None), P(), P(), P())
    out_specs = P("band", None)
    return jax.shard_map(shards, mesh=mesh, in_specs=in_specs, out_specs=out_specs, check_vma=False)
```

```python
import functools

import jax
import jax.numpy as jnp
from jax import lax
from jax.experimental import pallas as pl
from jax.experimental.pallas import tpu as pltpu
from jax.sharding import PartitionSpec as P

TILE = 128
HALF = 64
MIRROR_TILE = 64
PHASE_FACTOR = 4.0
F32 = jnp.float32
BF16 = jnp.bfloat16


def whole(*_):
    return pl.BlockSpec(memory_space=pltpu.VMEM)


def write_weights(tiles_ref, w_ref, split):
    for o in range(3):
        re = tiles_ref[o, 0].astype(F32)
        im = tiles_ref[o, 1].astype(F32)
        upper = jnp.concatenate([re, im], axis=1).astype(BF16)
        lower = jnp.concatenate([-im, re], axis=1).astype(BF16)
        if split:
            w_ref[o, 0:64] = upper[0:64]
            w_ref[o, 64:128] = lower[0:64]
            w_ref[o, 128:192] = upper[64:128]
            w_ref[o, 192:256] = lower[64:128]
        else:
            w_ref[o, 0:128] = upper
            w_ref[o, 128:256] = lower


def banded_rows(x_ref, w_ref, row, count, rows, flip=False):
    total = None
    for o in range(3):
        x = x_ref[pl.ds(pl.multiple_of(row + o * rows, 64), count)]
        if flip:
            part = lax.dot_general(x, w_ref[2 - o], (((1,), (1,)), ((), ())), preferred_element_type=F32)
        else:
            part = jnp.dot(x, w_ref[o], preferred_element_type=F32)
        total = part if total is None else total + part
    return total


def cos_sin(x):
    n = jnp.floor(x * 0.6366197723675814 + 0.5)
    r = x - n * 1.5703125
    r = r - n * 4.837512969970703e-4
    r = r - n * 7.549789948768648e-8
    r2 = r * r
    sin = r + r * r2 * (-1.6666654611e-1 + r2 * (8.3321608736e-3 - r2 * 1.9515295891e-4))
    cos = 1.0 - 0.5 * r2 + r2 * r2 * (4.166664568298827e-2 + r2 * (-1.388731625493765e-3 + r2 * 2.443315711809948e-5))
    quarter = n.astype(jnp.int32)
    odd = (quarter & 1) == 1
    cos_out = jnp.where(odd, sin, cos)
    sin_out = jnp.where(odd, cos, sin)
    return (
        jnp.where(((quarter + 1) & 2) != 0, -cos_out, cos_out),
        jnp.where((quarter & 2) != 0, -sin_out, sin_out),
    )


def first_kernel(field_ref, tiles_ref, footprint_ref, figure_ref, out_ref, field_buf, figure_buf, out_buf, wide_ref,
                 spread_ref, rows_ref, pick_ref, chunk_ref, x_ref, w_ref, in_sem, out_sem):
    count_tiles = field_ref.shape[0] // 128
    bands, blocks = footprint_ref.shape
    rows = 64
    pitch = 2 * count_tiles + 1
    parts = 4
    lines = rows // parts
    size = lines * 2 * count_tiles
    figure_load = pltpu.make_async_copy(figure_ref, figure_buf, in_sem.at[parts])
    figure_load.start()
    loads = [
        pltpu.make_async_copy(
            field_ref.at[pl.ds(i * size, size)], field_buf.at[pl.ds(i * size, size)], in_sem.at[i]
        )
        for i in range(parts)
    ]
    for load in loads:
        load.start()
    write_weights(tiles_ref, w_ref, False)
    x_ref[0:rows] = jnp.zeros((rows, 256), BF16)
    x_ref[(count_tiles + 1) * rows : (count_tiles + 2) * rows] = jnp.zeros((rows, 256), BF16)
    chunk_ref[pl.ds(9, 8 * bands, stride=10)] = jnp.zeros((8 * bands, 128), F32)

    mode, band = lax.axis_index("mode"), lax.axis_index("band")
    figure_load.wait()
    for p in range(blocks // 2):
        x = figure_buf[:, p * 128 : (p + 1) * 128].astype(F32)
        for g in range(8):
            spread_ref[pl.ds(p * 72 + g * 9, 8)] = x[g * 8 : (g + 1) * 8]
        mine = spread_ref[pl.ds(p * 72 + mode, 8, stride=9)]
        rows_ref[pl.ds(2 * p * 9, 8)] = mine
        rows_ref[pl.ds((2 * p + 1) * 9, 8)] = pltpu.roll(mine, 64, 1)
    for i in range(8):
        pick_ref[:, i * 128 : (i + 1) * 128] = rows_ref[pl.ds(i, blocks, stride=9)].astype(BF16)
    footprint = footprint_ref[...]
    column = lax.broadcasted_iota(jnp.int32, (bands, blocks), 1)
    code = (column * blocks + (footprint & (blocks - 1))).astype(F32)
    here = (footprint >> (blocks.bit_length() - 1)) == band
    low = jnp.min(jnp.where(here, code, float(blocks * blocks)), axis=1, keepdims=True).astype(jnp.int32)
    high = jnp.max(jnp.where(here, code, 0.0), axis=1, keepdims=True).astype(jnp.int32)
    picked = []
    for c, chosen in enumerate((low, high)):
        hot = column == ((chosen & (blocks - 1)) ^ c)
        hot = jnp.where(hot, 1.0, 0.0).astype(BF16)
        picked.append(jnp.dot(hot, pick_ref[...], preferred_element_type=F32))
    lane = lax.broadcasted_iota(jnp.int32, (bands, 128), 1)
    for i in range(8):
        at = slice(i * 128, (i + 1) * 128)
        chunk_ref[pl.ds(i * bands * 10 + 8, bands, stride=10)] = jnp.where(lane < 64, picked[0][:, at], picked[1][:, at])

    for u in range(rows):
        if u % lines == 0:
            loads[u // lines].wait()
        wide_ref[u * pitch : u * pitch + 2 * count_tiles] = field_buf[
            u * 2 * count_tiles : (u + 1) * 2 * count_tiles
        ].astype(F32)
    for j in range(count_tiles):
        for c in range(2):
            x_ref[(j + 1) * rows : (j + 2) * rows, c * 128 : (c + 1) * 128] = wide_ref[
                pl.ds(2 * j + c, rows, stride=pitch)
            ].astype(BF16)
    step = 16
    stores = []
    for q in range(count_tiles // step):
        got = banded_rows(x_ref, w_ref, q * (step * rows), step * rows, rows)
        for t in range(step):
            mine = got[t * rows : (t + 1) * rows]
            stacked = jnp.concatenate([mine[:, 0:128], mine[:, 128:256]], axis=0)
            turned = jnp.transpose(stacked)
            at = (q * step + t) * 2
            for h in range(2):
                for i in range(8):
                    from_row = h * 64 + i * 8
                    chunk_ref[pl.ds((i * bands + at + h) * 10, 8)] = turned[from_row : from_row + 8]
        span = 2 * step * 10
        for i in range(8):
            at = i * bands * 10 + q * span
            out_buf[at : at + span] = chunk_ref[at : at + span].astype(BF16)
            store = pltpu.make_async_copy(
                out_buf.at[pl.ds(at, span)], out_ref.at[pl.ds(at, span)], out_sem.at[q * 8 + i]
            )
            store.start()
            stores.append(store)
    for store in stores:
        store.wait()


def first_stage(field, tiles, footprint, figure):
    rows, length = field.shape[1], field.shape[3]
    count = length // TILE
    bands, blocks = footprint.shape
    field = field.reshape(rows, 2, count, TILE).transpose(0, 2, 1, 3).reshape(rows * count * 2, TILE)
    shape = (8 * bands * 10, TILE)
    return pl.pallas_call(
        first_kernel,
        out_shape=jax.ShapeDtypeStruct(shape, BF16),
        in_specs=[pl.BlockSpec(memory_space=pl.ANY), whole(), whole(), pl.BlockSpec(memory_space=pl.ANY)],
        out_specs=pl.BlockSpec(memory_space=pl.ANY),
        scratch_shapes=[
            pltpu.VMEM(field.shape, BF16),
            pltpu.VMEM(figure.shape, BF16),
            pltpu.VMEM(shape, BF16),
            pltpu.VMEM((rows * (2 * count + 1), 128), F32),
            pltpu.VMEM((blocks // 2 * 72, 128), F32),
            pltpu.VMEM((blocks * 9, 128), F32),
            pltpu.VMEM((blocks, 8 * 128), BF16),
            pltpu.VMEM(shape, F32),
            pltpu.VMEM(((count + 2) * rows, 256), BF16),
            pltpu.VMEM((3, 256, 256), BF16),
            pltpu.SemaphoreType.DMA((5,)),
            pltpu.SemaphoreType.DMA((8 * (count // 16),)),
        ],
        cost_estimate=pl.CostEstimate(flops=2 * rows * count * 768 * 256, bytes_accessed=1 << 21, transcendentals=0),
        name="first",
    )(field, tiles, footprint, figure)


def both_ways(wide_ref, at, x):
    wide_ref[2 * at] = x
    wide_ref[2 * at + 1] = pltpu.roll(x, 64, 1)


def second_kernel(index_ref, given_ref, approach_ref, focus_ref, target_ref, out_ref,
                  got_ref, wide_ref, turn_ref, heights_ref, want_ref, x_ref, y_ref, g_ref, wp_ref, wf_ref, sem):
    bands = out_ref.shape[0]
    pairs = bands // 2
    rows = 64
    parts = 4
    size = given_ref.shape[0] // parts
    loads = [
        pltpu.make_async_copy(given_ref.at[pl.ds(i * size, size)], got_ref.at[pl.ds(i * size, size)], sem.at[i])
        for i in range(parts)
    ]
    mode = lax.axis_index("mode")
    loads.append(
        pltpu.make_async_copy(target_ref.at[pl.ds(pl.multiple_of(mode * 8, 8), 8)], want_ref, sem.at[parts])
    )
    for load in loads:
        load.start()
    write_weights(approach_ref, wp_ref, True)
    write_weights(focus_ref, wf_ref, False)
    blank = jnp.zeros((rows, 256), BF16)
    for ref in (x_ref, y_ref, g_ref):
        ref[0:rows] = blank
        ref[(pairs + 1) * rows : (pairs + 2) * rows] = blank
    for i in range(parts):
        loads[i].wait()
        wide_ref[i * size : (i + 1) * size] = got_ref[i * size : (i + 1) * size].astype(F32)
    loads[parts].wait()

    for p in range(pairs):
        for h in range(2):
            x = [wide_ref[pl.ds((m * bands + 2 * p + h) * 10, 8)] for m in range(8)]
            x_ref[(p + 1) * rows : (p + 2) * rows, h * 128 : (h + 1) * 128] = jnp.concatenate(x, axis=0).astype(BF16)
    for m in range(8):
        for g in range(bands // 8):
            at = (m * bands + 8 * g) * 10 + 8
            turn_ref[pl.ds(8 * g * 9 + m, 8, stride=9)] = wide_ref[pl.ds(at, 8, stride=10)]
    for s in range(bands):
        both_ways(heights_ref, s, turn_ref[pl.ds(9 * s, 8)])
    lane = lax.broadcasted_iota(jnp.int32, (8, 128), 1)
    step = 16

    def mirror(q, carry):
        row = q * (step * rows)
        a2 = banded_rows(x_ref, wp_ref, row, step * rows, rows).astype(BF16).astype(F32)
        re = a2[:, 0:128].reshape(step, 8, 8, 128)
        im = a2[:, 128:256].reshape(step, 8, 8, 128)
        waves = []
        for t in range(step):
            a = heights_ref[index_ref[2, 2 * (q * step + t)]]
            b = heights_ref[index_ref[2, 2 * (q * step + t) + 1]]
            waves.append(cos_sin(PHASE_FACTOR * jnp.where(lane < 64, a, b)))
        cos = jnp.stack([wave[0] for wave in waves])[:, None]
        sin = jnp.stack([wave[1] for wave in waves])[:, None]
        to = pl.ds(pl.multiple_of(row + rows, 64), step * rows)
        y_ref[to, 0:128] = (re * cos - im * sin).reshape(step * rows, 128).astype(BF16)
        y_ref[to, 128:256] = (re * sin + im * cos).reshape(step * rows, 128).astype(BF16)
        return carry

    lax.fori_loop(0, pairs // step, mirror, 0)

    def detect(q, carry):
        row = q * (step * rows)
        a4 = banded_rows(y_ref, wf_ref, row, step * rows, rows)
        re = a4[:, 0:128].reshape(step, 8, 8, 128)
        im = a4[:, 128:256].reshape(step, 8, 8, 128)
        power = jnp.sum(re * re + im * im, axis=1)
        to = pl.ds(pl.multiple_of(row + rows, 64), step * rows)
        for t in range(step):
            at = pl.ds(pl.multiple_of((q * step + t) * 128, 128), 128)
            left = (power[t] - want_ref[:, at].astype(F32))[None]
            to = pl.ds(pl.multiple_of(row + rows + t * rows, 64), rows)
            g_ref[to, 0:128] = (re[t] * left).reshape(rows, 128).astype(BF16)
            g_ref[to, 128:256] = (im[t] * left).reshape(rows, 128).astype(BF16)
        return carry

    lax.fori_loop(0, pairs // step, detect, 0)
    out_ref[...] = jnp.zeros_like(out_ref)

    def adjoint(q, carry):
        row = q * (step * rows)
        g3 = banded_rows(g_ref, wf_ref, row, step * rows, rows, flip=True)
        own = pl.ds(pl.multiple_of(row + rows, 64), step * rows)
        re = y_ref[own, 0:128].astype(F32)
        im = y_ref[own, 128:256].astype(F32)
        terms = g3[:, 128:256] * re - g3[:, 0:128] * im
        sens = 2.0 * PHASE_FACTOR * jnp.sum(terms.reshape(step, 8, 8, 128), axis=1)
        for t in range(step):
            turned = pltpu.roll(sens[t], 64, 1)
            for h in range(2):
                j = (q * step + t) * 2 + h
                s, c = index_ref[0, j], index_ref[1, j]
                tile = jnp.where(c != h, turned, sens[t])
                out_ref[s] = jnp.where((lane < 64) == (c == 0), tile, out_ref[s].astype(F32)).astype(BF16)
        return carry

    lax.fori_loop(0, pairs // step, adjoint, 0)


def second_stage(index, got, approach, focus, target, bands):
    pairs = bands // 2
    anywhere = pl.BlockSpec(memory_space=pl.ANY)
    return pl.pallas_call(
        second_kernel,
        out_shape=jax.ShapeDtypeStruct((bands, 8, 128), BF16),
        in_specs=[pl.BlockSpec(memory_space=pltpu.SMEM), anywhere, whole(), whole(), anywhere],
        out_specs=whole(),
        scratch_shapes=[
            pltpu.VMEM(got.shape, BF16),
            pltpu.VMEM(got.shape, F32),
            pltpu.VMEM((9 * bands, 128), F32),
            pltpu.VMEM((2 * bands, 8, 128), F32),
            pltpu.VMEM((8, target.shape[1]), BF16),
        ]
        + [pltpu.VMEM(((pairs + 2) * 64, 256), BF16)] * 3
        + [pltpu.VMEM((3, 256, 256), BF16)] * 2
        + [pltpu.SemaphoreType.DMA((5,))],
        cost_estimate=pl.CostEstimate(flops=6 * 64 * pairs * 768 * 256, bytes_accessed=1 << 20, transcendentals=0),
        compiler_params=pltpu.CompilerParams(vmem_limit_bytes=32 << 20),
        name="second",
    )(index, got, approach, focus, target)


def collect_kernel(index_ref, given_ref, out_ref, tiles_ref, wide_ref, sem, *sums):
    lane = lax.broadcasted_iota(jnp.int32, (8, 128), 1)
    pairs = out_ref.shape[1] // 128
    bands = tiles_ref.shape[0]
    load = pltpu.make_async_copy(given_ref, tiles_ref, sem)
    load.start()
    for part in sums:
        part[...] = jnp.zeros_like(part)
    load.wait()
    for d in range(bands):
        both_ways(wide_ref, d, tiles_ref[d].astype(F32))
    for d in range(bands):
        for c in range(2):
            part = sums[2 * (d % 2) + c]
            k = index_ref[c, d]
            part[k] += wide_ref[2 * d + ((k & 1) ^ c)]
    for p in range(pairs):
        low = sums[0][2 * p] + sums[1][2 * p] + sums[2][2 * p] + sums[3][2 * p]
        high = sums[0][2 * p + 1] + sums[1][2 * p + 1] + sums[2][2 * p + 1] + sums[3][2 * p + 1]
        out_ref[:, p * 128 : (p + 1) * 128] = jnp.where(lane < 64, low, high).astype(out_ref.dtype)


def collect(index, tiles, dtype):
    bands = tiles.shape[0]
    return pl.pallas_call(
        collect_kernel,
        out_shape=jax.ShapeDtypeStruct((8, bands * 64), dtype),
        in_specs=[pl.BlockSpec(memory_space=pltpu.SMEM), pl.BlockSpec(memory_space=pl.ANY)],
        out_specs=whole(),
        scratch_shapes=[
            pltpu.VMEM(tiles.shape, BF16),
            pltpu.VMEM((2 * bands, 8, 128), F32),
            pltpu.SemaphoreType.DMA,
        ]
        + [pltpu.VMEM((bands + 8, 8, 128), F32)] * 4,
        compiler_params=pltpu.CompilerParams(vmem_limit_bytes=8 << 20),
        name="collect",
    )(index, tiles)


def shards(mode_field, figure, target, footprint, approach_tiles, focus_tiles):
    band = lax.axis_index("band").astype(jnp.int32)
    bands, blocks = footprint.shape
    out = first_stage(mode_field, approach_tiles, footprint, figure)
    sent = out.reshape(-1, 5, 2, TILE).transpose(0, 2, 1, 3).reshape(-1, 2, 5 * TILE)
    got = lax.all_to_all(sent, ("mode", "band"), split_axis=0, concat_axis=0, tiled=True)
    got = got.reshape(-1, 2, 5, TILE).transpose(0, 2, 1, 3).reshape(out.shape)
    source_band = lax.div(footprint, blocks)
    code = lax.broadcasted_iota(jnp.int32, footprint.shape, 1) * blocks + lax.rem(footprint, blocks)
    here = source_band == band
    low = jnp.min(jnp.where(here, code, blocks * blocks), axis=1)
    high = jnp.max(jnp.where(here, code, -1), axis=1)
    add_index = jnp.stack(
        [
            jnp.where(high >= 0, low & (blocks - 1), blocks),
            jnp.where(high > low, high & (blocks - 1), blocks),
        ]
    )
    my_band = lax.dynamic_index_in_dim(source_band, band, 0, keepdims=False)
    column = jnp.arange(blocks, dtype=jnp.int32)
    same = (my_band[:, None] == my_band[None, :]) & (column[None, :] < column[:, None])
    my_slot = jnp.any(same, axis=1).astype(jnp.int32)
    beam_index = jnp.stack([my_band, my_slot, 2 * my_band + (my_slot ^ (column & 1))])
    tiles = second_stage(beam_index, got, approach_tiles, focus_tiles, target, bands)
    tiles = lax.all_to_all(tiles, "band", split_axis=0, concat_axis=0, tiled=True)
    own = collect(add_index, tiles, BF16)
    return lax.all_gather(own, "mode", axis=0, tiled=True).astype(F32)


def solution(mesh):
    in_specs = (P("mode", "band", None, None), P("band", None), P("band", None), P(), P(), P())
    out_specs = P("band", None)
    return jax.shard_map(shards, mesh=mesh, in_specs=in_specs, out_specs=out_specs, check_vma=False)
```

```python
import functools

import jax
import jax.numpy as jnp
from jax import lax
from jax.experimental import pallas as pl
from jax.experimental.pallas import tpu as pltpu
from jax.sharding import PartitionSpec as P

TILE = 128
HALF = 64
MIRROR_TILE = 64
PHASE_FACTOR = 4.0
F32 = jnp.float32
BF16 = jnp.bfloat16


def whole(*_):
    return pl.BlockSpec(memory_space=pltpu.VMEM)


def write_weights(tiles_ref, w_ref, split):
    for o in range(3):
        re = tiles_ref[o, 0].astype(F32)
        im = tiles_ref[o, 1].astype(F32)
        upper = jnp.concatenate([re, im], axis=1).astype(BF16)
        lower = jnp.concatenate([-im, re], axis=1).astype(BF16)
        if split:
            w_ref[o, 0:64] = upper[0:64]
            w_ref[o, 64:128] = lower[0:64]
            w_ref[o, 128:192] = upper[64:128]
            w_ref[o, 192:256] = lower[64:128]
        else:
            w_ref[o, 0:128] = upper
            w_ref[o, 128:256] = lower


def banded_rows(x_ref, w_ref, row, count, rows, flip=False):
    total = None
    for o in range(3):
        x = x_ref[pl.ds(pl.multiple_of(row + o * rows, 64), count)]
        if flip:
            part = lax.dot_general(x, w_ref[2 - o], (((1,), (1,)), ((), ())), preferred_element_type=F32)
        else:
            part = jnp.dot(x, w_ref[o], preferred_element_type=F32)
        total = part if total is None else total + part
    return total


def cos_sin(x):
    n = jnp.floor(x * 0.6366197723675814 + 0.5)
    r = x - n * 1.5703125
    r = r - n * 4.837512969970703e-4
    r = r - n * 7.549789948768648e-8
    r2 = r * r
    sin = r + r * r2 * (-1.6666654611e-1 + r2 * (8.3321608736e-3 - r2 * 1.9515295891e-4))
    cos = 1.0 - 0.5 * r2 + r2 * r2 * (4.166664568298827e-2 + r2 * (-1.388731625493765e-3 + r2 * 2.443315711809948e-5))
    quarter = n.astype(jnp.int32)
    odd = (quarter & 1) == 1
    cos_out = jnp.where(odd, sin, cos)
    sin_out = jnp.where(odd, cos, sin)
    return (
        jnp.where(((quarter + 1) & 2) != 0, -cos_out, cos_out),
        jnp.where((quarter & 2) != 0, -sin_out, sin_out),
    )


def first_kernel(field_ref, tiles_hbm, footprint_hbm, figure_ref, out_ref, tiles_ref, footprint_ref, field_buf,
                 figure_buf, out_buf, wide_ref, spread_ref, rows_ref, pick_ref, chunk_ref, x_ref, w_ref, in_sem, out_sem):
    count_tiles = field_ref.shape[0] // 128
    bands, blocks = footprint_ref.shape
    rows = 64
    pitch = 2 * count_tiles + 1
    parts = 4
    lines = rows // parts
    size = lines * 2 * count_tiles
    tiles_load = pltpu.make_async_copy(tiles_hbm, tiles_ref, in_sem.at[parts + 1])
    footprint_load = pltpu.make_async_copy(footprint_hbm, footprint_ref, in_sem.at[parts + 2])
    figure_load = pltpu.make_async_copy(figure_ref, figure_buf, in_sem.at[parts])
    for load in (tiles_load, footprint_load, figure_load):
        load.start()
    loads = [
        pltpu.make_async_copy(
            field_ref.at[pl.ds(i * size, size)], field_buf.at[pl.ds(i * size, size)], in_sem.at[i]
        )
        for i in range(parts)
    ]
    for load in loads:
        load.start()
    x_ref[0:rows] = jnp.zeros((rows, 256), BF16)
    x_ref[(count_tiles + 1) * rows : (count_tiles + 2) * rows] = jnp.zeros((rows, 256), BF16)
    chunk_ref[pl.ds(9, 8 * bands, stride=10)] = jnp.zeros((8 * bands, 128), F32)
    tiles_load.wait()
    write_weights(tiles_ref, w_ref, False)

    mode, band = lax.axis_index("mode"), lax.axis_index("band")
    footprint_load.wait()
    figure_load.wait()
    for p in range(blocks // 2):
        x = figure_buf[:, p * 128 : (p + 1) * 128].astype(F32)
        for g in range(8):
            spread_ref[pl.ds(p * 72 + g * 9, 8)] = x[g * 8 : (g + 1) * 8]
        mine = spread_ref[pl.ds(p * 72 + mode, 8, stride=9)]
        rows_ref[pl.ds(2 * p * 9, 8)] = mine
        rows_ref[pl.ds((2 * p + 1) * 9, 8)] = pltpu.roll(mine, 64, 1)
    for i in range(8):
        pick_ref[:, i * 128 : (i + 1) * 128] = rows_ref[pl.ds(i, blocks, stride=9)].astype(BF16)
    footprint = footprint_ref[...]
    column = lax.broadcasted_iota(jnp.int32, (bands, blocks), 1)
    code = (column * blocks + (footprint & (blocks - 1))).astype(F32)
    here = (footprint >> (blocks.bit_length() - 1)) == band
    low = jnp.min(jnp.where(here, code, float(blocks * blocks)), axis=1, keepdims=True).astype(jnp.int32)
    high = jnp.max(jnp.where(here, code, 0.0), axis=1, keepdims=True).astype(jnp.int32)
    picked = []
    for c, chosen in enumerate((low, high)):
        hot = column == ((chosen & (blocks - 1)) ^ c)
        hot = jnp.where(hot, 1.0, 0.0).astype(BF16)
        picked.append(jnp.dot(hot, pick_ref[...], preferred_element_type=F32))
    lane = lax.broadcasted_iota(jnp.int32, (bands, 128), 1)
    for i in range(8):
        at = slice(i * 128, (i + 1) * 128)
        chunk_ref[pl.ds(i * bands * 10 + 8, bands, stride=10)] = jnp.where(lane < 64, picked[0][:, at], picked[1][:, at])

    for u in range(rows):
        if u % lines == 0:
            loads[u // lines].wait()
        wide_ref[u * pitch : u * pitch + 2 * count_tiles] = field_buf[
            u * 2 * count_tiles : (u + 1) * 2 * count_tiles
        ].astype(F32)
    for j in range(count_tiles):
        for c in range(2):
            x_ref[(j + 1) * rows : (j + 2) * rows, c * 128 : (c + 1) * 128] = wide_ref[
                pl.ds(2 * j + c, rows, stride=pitch)
            ].astype(BF16)
    step = 16
    stores = []
    for q in range(count_tiles // step):
        got = banded_rows(x_ref, w_ref, q * (step * rows), step * rows, rows)
        for t in range(step):
            mine = got[t * rows : (t + 1) * rows]
            stacked = jnp.concatenate([mine[:, 0:128], mine[:, 128:256]], axis=0)
            turned = jnp.transpose(stacked)
            at = (q * step + t) * 2
            for h in range(2):
                for i in range(8):
                    from_row = h * 64 + i * 8
                    chunk_ref[pl.ds((i * bands + at + h) * 10, 8)] = turned[from_row : from_row + 8]
        span = 2 * step * 10
        for i in range(8):
            at = i * bands * 10 + q * span
            out_buf[at : at + span] = chunk_ref[at : at + span].astype(BF16)
            store = pltpu.make_async_copy(
                out_buf.at[pl.ds(at, span)], out_ref.at[pl.ds(at, span)], out_sem.at[q * 8 + i]
            )
            store.start()
            stores.append(store)
    for store in stores:
        store.wait()


def first_stage(field, tiles, footprint, figure):
    rows, length = field.shape[1], field.shape[3]
    count = length // TILE
    bands, blocks = footprint.shape
    field = field.reshape(rows, 2, count, TILE).transpose(0, 2, 1, 3).reshape(rows * count * 2, TILE)
    shape = (8 * bands * 10, TILE)
    return pl.pallas_call(
        first_kernel,
        out_shape=jax.ShapeDtypeStruct(shape, BF16),
        in_specs=[pl.BlockSpec(memory_space=pl.ANY)] * 4,
        out_specs=pl.BlockSpec(memory_space=pl.ANY),
        scratch_shapes=[
            pltpu.VMEM(tiles.shape, BF16),
            pltpu.VMEM(footprint.shape, jnp.int32),
            pltpu.VMEM(field.shape, BF16),
            pltpu.VMEM(figure.shape, BF16),
            pltpu.VMEM(shape, BF16),
            pltpu.VMEM(((rows + 1) * (2 * count + 1) + 7, 128), F32),
            pltpu.VMEM(((blocks // 2 + 1) * 72, 128), F32),
            pltpu.VMEM((blocks * 9 + 16, 128), F32),
            pltpu.VMEM((blocks, 8 * 128), BF16),
            pltpu.VMEM((shape[0] + 16, 128), F32),
            pltpu.VMEM(((count + 2) * rows, 256), BF16),
            pltpu.VMEM((3, 256, 256), BF16),
            pltpu.SemaphoreType.DMA((7,)),
            pltpu.SemaphoreType.DMA((8 * (count // 16),)),
        ],
        cost_estimate=pl.CostEstimate(flops=2 * rows * count * 768 * 256, bytes_accessed=1 << 21, transcendentals=0),
        name="first",
    )(field, tiles, footprint, figure)


def both_ways(wide_ref, at, x):
    wide_ref[2 * at] = x
    wide_ref[2 * at + 1] = pltpu.roll(x, 64, 1)


def second_kernel(index_ref, got_ref, approach_ref, focus_ref, target_ref, out_ref, wide_ref,
                  turn_ref, heights_ref, want_ref, x_ref, y_ref, g_ref, wp_ref, wf_ref, sem):
    bands = out_ref.shape[0]
    pairs = bands // 2
    rows = 64
    mode = lax.axis_index("mode")
    load = pltpu.make_async_copy(target_ref.at[pl.ds(pl.multiple_of(mode * 8, 8), 8)], want_ref, sem)
    load.start()
    write_weights(approach_ref, wp_ref, True)
    write_weights(focus_ref, wf_ref, False)
    blank = jnp.zeros((rows, 256), BF16)
    for ref in (x_ref, y_ref, g_ref):
        ref[0:rows] = blank
        ref[(pairs + 1) * rows : (pairs + 2) * rows] = blank
    wide_ref[0 : got_ref.shape[0]] = got_ref[...].astype(F32)
    load.wait()

    for p in range(pairs):
        for h in range(2):
            x = [wide_ref[pl.ds((m * bands + 2 * p + h) * 10, 8)] for m in range(8)]
            x_ref[(p + 1) * rows : (p + 2) * rows, h * 128 : (h + 1) * 128] = jnp.concatenate(x, axis=0).astype(BF16)
    for m in range(8):
        for g in range(bands // 8):
            at = (m * bands + 8 * g) * 10 + 8
            turn_ref[pl.ds(8 * g * 9 + m, 8, stride=9)] = wide_ref[pl.ds(at, 8, stride=10)]
    for s in range(bands):
        both_ways(heights_ref, s, turn_ref[pl.ds(9 * s, 8)])
    lane = lax.broadcasted_iota(jnp.int32, (8, 128), 1)
    step = 16

    def mirror(q, carry):
        row = q * (step * rows)
        a2 = banded_rows(x_ref, wp_ref, row, step * rows, rows).astype(BF16).astype(F32)
        re = a2[:, 0:128].reshape(step, 8, 8, 128)
        im = a2[:, 128:256].reshape(step, 8, 8, 128)
        waves = []
        for t in range(step):
            a = heights_ref[index_ref[2, 2 * (q * step + t)]]
            b = heights_ref[index_ref[2, 2 * (q * step + t) + 1]]
            waves.append(cos_sin(PHASE_FACTOR * jnp.where(lane < 64, a, b)))
        cos = jnp.stack([wave[0] for wave in waves])[:, None]
        sin = jnp.stack([wave[1] for wave in waves])[:, None]
        to = pl.ds(pl.multiple_of(row + rows, 64), step * rows)
        y_ref[to, 0:128] = (re * cos - im * sin).reshape(step * rows, 128).astype(BF16)
        y_ref[to, 128:256] = (re * sin + im * cos).reshape(step * rows, 128).astype(BF16)
        return carry

    lax.fori_loop(0, pairs // step, mirror, 0)

    def detect(q, carry):
        row = q * (step * rows)
        a4 = banded_rows(y_ref, wf_ref, row, step * rows, rows)
        re = a4[:, 0:128].reshape(step, 8, 8, 128)
        im = a4[:, 128:256].reshape(step, 8, 8, 128)
        power = jnp.sum(re * re + im * im, axis=1)
        to = pl.ds(pl.multiple_of(row + rows, 64), step * rows)
        for t in range(step):
            at = pl.ds(pl.multiple_of((q * step + t) * 128, 128), 128)
            left = (power[t] - want_ref[:, at].astype(F32))[None]
            to = pl.ds(pl.multiple_of(row + rows + t * rows, 64), rows)
            g_ref[to, 0:128] = (re[t] * left).reshape(rows, 128).astype(BF16)
            g_ref[to, 128:256] = (im[t] * left).reshape(rows, 128).astype(BF16)
        return carry

    lax.fori_loop(0, pairs // step, detect, 0)
    out_ref[...] = jnp.zeros_like(out_ref)

    def adjoint(q, carry):
        row = q * (step * rows)
        g3 = banded_rows(g_ref, wf_ref, row, step * rows, rows, flip=True)
        own = pl.ds(pl.multiple_of(row + rows, 64), step * rows)
        re = y_ref[own, 0:128].astype(F32)
        im = y_ref[own, 128:256].astype(F32)
        terms = g3[:, 128:256] * re - g3[:, 0:128] * im
        sens = 2.0 * PHASE_FACTOR * jnp.sum(terms.reshape(step, 8, 8, 128), axis=1)
        for t in range(step):
            turned = pltpu.roll(sens[t], 64, 1)
            for h in range(2):
                j = (q * step + t) * 2 + h
                s, c = index_ref[0, j], index_ref[1, j]
                tile = jnp.where(c != h, turned, sens[t])
                out_ref[s] = jnp.where((lane < 64) == (c == 0), tile, out_ref[s].astype(F32)).astype(BF16)
        return carry

    lax.fori_loop(0, pairs // step, adjoint, 0)


def second_stage(index, got, approach, focus, target, bands):
    pairs = bands // 2
    anywhere = pl.BlockSpec(memory_space=pl.ANY)
    return pl.pallas_call(
        second_kernel,
        out_shape=jax.ShapeDtypeStruct((bands, 8, 128), BF16),
        in_specs=[pl.BlockSpec(memory_space=pltpu.SMEM), whole(), whole(), whole(), anywhere],
        out_specs=whole(),
        scratch_shapes=[
            pltpu.VMEM((got.shape[0] + 16, 128), F32),
            pltpu.VMEM((9 * bands + 16, 128), F32),
            pltpu.VMEM((2 * bands, 8, 128), F32),
            pltpu.VMEM((8, target.shape[1]), BF16),
        ]
        + [pltpu.VMEM(((pairs + 2) * 64, 256), BF16)] * 3
        + [pltpu.VMEM((3, 256, 256), BF16)] * 2
        + [pltpu.SemaphoreType.DMA],
        cost_estimate=pl.CostEstimate(flops=6 * 64 * pairs * 768 * 256, bytes_accessed=1 << 20, transcendentals=0),
        compiler_params=pltpu.CompilerParams(vmem_limit_bytes=32 << 20),
        name="second",
    )(index, got, approach, focus, target)


def collect_kernel(index_ref, tiles_ref, out_ref, wide_ref, *sums):
    lane = lax.broadcasted_iota(jnp.int32, (8, 128), 1)
    pairs = out_ref.shape[1] // 128
    bands = tiles_ref.shape[0]
    for part in sums:
        part[...] = jnp.zeros_like(part)
    for d in range(bands):
        both_ways(wide_ref, d, tiles_ref[d].astype(F32))
    for d in range(bands):
        for c in range(2):
            part = sums[2 * (d % 2) + c]
            k = index_ref[c, d]
            part[k] += wide_ref[2 * d + ((k & 1) ^ c)]
    for p in range(pairs):
        low = sums[0][2 * p] + sums[1][2 * p] + sums[2][2 * p] + sums[3][2 * p]
        high = sums[0][2 * p + 1] + sums[1][2 * p + 1] + sums[2][2 * p + 1] + sums[3][2 * p + 1]
        out_ref[:, p * 128 : (p + 1) * 128] = jnp.where(lane < 64, low, high).astype(out_ref.dtype)


def collect(index, tiles, dtype):
    bands = tiles.shape[0]
    return pl.pallas_call(
        collect_kernel,
        out_shape=jax.ShapeDtypeStruct((8, bands * 64), dtype),
        in_specs=[pl.BlockSpec(memory_space=pltpu.SMEM), whole()],
        out_specs=whole(),
        scratch_shapes=[pltpu.VMEM((2 * bands, 8, 128), F32)]
        + [pltpu.VMEM((bands + 8, 8, 128), F32)] * 4,
        compiler_params=pltpu.CompilerParams(vmem_limit_bytes=8 << 20),
        name="collect",
    )(index, tiles)


def shards(mode_field, figure, target, footprint, approach_tiles, focus_tiles):
    band = lax.axis_index("band").astype(jnp.int32)
    bands, blocks = footprint.shape
    out = first_stage(mode_field, approach_tiles, footprint, figure)
    sent = out.reshape(-1, 5, 2, TILE).transpose(0, 2, 1, 3).reshape(-1, 2, 5 * TILE)
    got = lax.all_to_all(sent, ("mode", "band"), split_axis=0, concat_axis=0, tiled=True)
    got = got.reshape(-1, 2, 5, TILE).transpose(0, 2, 1, 3).reshape(out.shape)
    source_band = lax.div(footprint, blocks)
    code = lax.broadcasted_iota(jnp.int32, footprint.shape, 1) * blocks + lax.rem(footprint, blocks)
    here = source_band == band
    low = jnp.min(jnp.where(here, code, blocks * blocks), axis=1)
    high = jnp.max(jnp.where(here, code, -1), axis=1)
    add_index = jnp.stack(
        [
            jnp.where(high >= 0, low & (blocks - 1), blocks),
            jnp.where(high > low, high & (blocks - 1), blocks),
        ]
    )
    my_band = lax.dynamic_index_in_dim(source_band, band, 0, keepdims=False)
    column = jnp.arange(blocks, dtype=jnp.int32)
    same = (my_band[:, None] == my_band[None, :]) & (column[None, :] < column[:, None])
    my_slot = jnp.any(same, axis=1).astype(jnp.int32)
    beam_index = jnp.stack([my_band, my_slot, 2 * my_band + (my_slot ^ (column & 1))])
    tiles = second_stage(beam_index, got, approach_tiles, focus_tiles, target, bands)
    tiles = lax.all_to_all(tiles, "band", split_axis=0, concat_axis=0, tiled=True)
    own = collect(add_index, tiles, BF16)
    return lax.all_gather(own, "mode", axis=0, tiled=True).astype(F32)


def solution(mesh):
    in_specs = (P("mode", "band", None, None), P("band", None), P("band", None), P(), P(), P())
    out_specs = P("band", None)
    return jax.shard_map(shards, mesh=mesh, in_specs=in_specs, out_specs=out_specs, check_vma=False)
```
